32 devices in a mesh: ctx: 8 (over z, y), head: 4 (over x, core).
Axes of the slice: x: 2, y: 2, z: 4, core: 2. Of those that a mesh axis runs over, the one named last changes fastest.
Arguments:
- queries: bfloat16 [4096, 4096], P('ctx', 'head'), may hold values from -6 to 6
- keys: bfloat16 [4096, 4096], P('ctx', 'head'), may hold values from -6 to 6
- values: bfloat16 [4096, 4096], P('ctx', 'head'), may hold values from -6 to 6
- cotangent: bfloat16 [4096, 4096], P('ctx', 'head'), may hold values from -6 to 6
- out_weight: bfloat16 [4096, 4096], P('head', 'ctx'), may hold values from -0.125 to 0.125
- level_table: float32 [16, 32, 8], P(None, 'head'), may hold values from 0.25 to 2
- table_index: int32 [4096], P('ctx'), may hold values from 0 to 15
- level_column: int32 [24], replicated, may hold values from 0 to 7, as said below
Outputs:
- layer_out: bfloat16 [4096, 4096], P('ctx', 'head')
- grad_queries: bfloat16 [4096, 4096], P('ctx', 'head')
- grad_keys: bfloat16 [4096, 4096], P('ctx', 'head')
- grad_values: bfloat16 [4096, 4096], P('ctx', 'head')
- grad_weight: float32 [4096, 4096], P('head', 'ctx')
The draws below stay inside these ranges and needn't reach their ends.
Inputs may be any that keep to these rules, and one draw needn't show every extreme that they name: `table_index`: a table number for every token. `level_column`: each of the 8 column numbers appears exactly 24 // 8 times; only the first 13 entries are used.
All inputs are finite; a program needn't handle non-finite values.
Results may differ from the reference program's by a relative error of at most 0.017.
Values may be sent and summed in bfloat16 or wider, within the bound.
No kernel may reach another device: no remote copies, remote signals or barrier semaphores. Data moves between devices by JAX's collectives and lax.ppermute only.
A program may use at most 128 MiB of HBM per device.

```python
import math
import jax
import jax.numpy as jnp
from jax import lax

D = 4096
H = 32
HD = 128
TOK_DEV = 512
NTAB = 16
NCOL = 8
MAXLEV = 24
TOKENS = 4096
TOK_BITS = 9
CTX_BITS = 3
LEVELS = 13
N_CTX = 8
N_HEAD = 4


def draw_level_column(key, part):
    return (jax.random.permutation(key, MAXLEV) % NCOL).astype(jnp.int32)


def plant(drawn, stream_key, least, high):
    longest = drawn.shape.index(max(drawn.shape))
    spots = []
    for shift in (0, 1):
        where = [jax.random.randint(jax.random.fold_in(stream_key, axis), (), 0, length) for axis, length in enumerate(drawn.shape)]
        where[longest] = (where[longest] + shift) % drawn.shape[longest]
        spots.append(tuple(where))
    return drawn.at[spots[0]].set(least).at[spots[1]].set(high)


def strengthened(entries, rng, source, target, blocks, factor):
    def block_of(position):
        return (jnp.arange(entries.shape[position]) // (entries.shape[position] // blocks)).reshape((-1,) + (1,) * (entries.ndim - 1 - position))

    one_side = jax.random.permutation(rng, blocks)[block_of(target)]
    other_side = (block_of(target) + blocks // 2) % blocks
    return jnp.where((block_of(source) == one_side) | (block_of(source) == other_side), factor * entries, entries)


def steps_of(rng, dims, cuts, low, top_value):
    factor_of = 1.0
    for position, blocks in cuts:
        heights = jax.random.uniform(jax.random.fold_in(jax.random.fold_in(rng, 6), position), (blocks,), jnp.float32, low / len(cuts), top_value / len(cuts))
        factor_of = factor_of * jnp.repeat(jnp.exp(heights), dims[position] // blocks).reshape((-1,) + (1,) * (len(dims) - 1 - position))
    return factor_of


def scatter_about(rng, extent, spread, most, pieces=(), held_as=jnp.bfloat16):
    level = steps_of(rng, extent, pieces, -0.22, 0.18) if pieces else 1.0
    drawn = jax.random.normal(rng, extent, jnp.float32) * spread * level
    return jnp.minimum(jnp.maximum(drawn, -most), most).astype(held_as)


def heavy_noise(stream_key, extent, spread, most, shards, heavy, kind=jnp.bfloat16):
    values = spread * jax.random.normal(stream_key, extent, jnp.float32)
    if shards:
        values = values * steps_of(stream_key, extent, shards, -0.22, 0.18)
    return jnp.clip(strengthened(values, jax.random.fold_in(stream_key, 3), *heavy), -most, most).astype(kind)


def setup_inputs(seed: int = 0) -> dict:
    seeds = jax.random.split(jax.random.key(seed), 9)
    return {
        "queries": scatter_about(seeds[0], (TOKENS, H * HD), 1.0, 6.0, ((0, 8), (1, 4))),
        "keys": scatter_about(seeds[1], (TOKENS, H * HD), 1.0, 6.0, ((0, 8), (1, 4))),
        "values": scatter_about(seeds[2], (TOKENS, H * HD), 1.0, 6.0, ((0, 8), (1, 4))),
        "cotangent": heavy_noise(seeds[3], (TOKENS, D), 1.0, 6.0, ((0, 8), (1, 4)), (0, 1, 8, 2.0)),
        "out_weight": heavy_noise(seeds[4], (H * HD, D), (H * HD) ** -0.5, 0.125, ((0, 4), (1, 8)), (0, 1, 8, 2.0)),
        "level_table": jnp.clip(jnp.exp(math.log(2.0) - 2.0794415 * jax.random.uniform(seeds[5], (NTAB, H, NCOL), jnp.float32) ** steps_of(seeds[5], (NTAB, H, NCOL), ((1, 4),), -0.2, 0.2)), 0.25, 2.0),
        "table_index": plant(jax.random.randint(seeds[6], (TOKENS,), 0, NTAB), jax.random.fold_in(seeds[6], 1), 0, NTAB - 1).astype(jnp.int32),
        "level_column": draw_level_column(jax.random.fold_in(seeds[8], 71), 0),
    }


def level_scales(levels):
    level_ids = jnp.arange(levels, dtype=jnp.float32)
    return jnp.where(level_ids < 0.5, 1.0, jnp.exp2(-(level_ids - 1.0) * 0.5)).astype(jnp.float32)


def token_levels(tok_rows, tok_bits):
    positions = jnp.arange(tok_rows, dtype=jnp.int32)
    xor_pos = jnp.bitwise_xor(positions[:, None], positions[None, :])
    level_map = jnp.zeros((tok_rows, tok_rows), jnp.int32)
    for step_bit in range(tok_bits):
        level_map = level_map + (xor_pos >= (1 << step_bit)).astype(jnp.int32)
    return level_map, positions[None, :] <= positions[:, None]


def block_weights(near_weight, level_map, causal, qk_scale):
    head_count, tok_rows, near_count = near_weight.shape
    running_sum = jnp.zeros((head_count, tok_rows, tok_rows), jnp.float32)
    for level_id in range(near_count):
        running_sum = running_sum + jnp.where((level_map == level_id)[None], near_weight[:, :, level_id][:, :, None], 0.0)
    return jnp.where(causal[None], qk_scale * running_sum, 0.0)


def reference(queries, keys, values, cotangent, out_weight, level_table, table_index, level_column):
    f32 = jnp.float32
    high = lax.Precision.HIGHEST
    qk_scale = HD ** -0.5
    level_weight = level_table[table_index][:, :, level_column[:LEVELS]] * level_scales(LEVELS)[None, None, :]
    level_map, causal = token_levels(TOK_DEV, TOK_BITS)
    grad_attn = lax.dot_general(cotangent, out_weight, (((1,), (1,)), ((), ())), preferred_element_type=f32).astype(jnp.bfloat16)

    def split_blocks(array):
        return array.reshape(N_CTX, TOK_DEV, H, HD)

    block_ids = jnp.arange(N_CTX, dtype=jnp.int32)
    bit_table = ((block_ids[:, None] >> jnp.arange(CTX_BITS, dtype=jnp.int32)[None, :]) & 1).astype(f32)
    items = (split_blocks(queries), split_blocks(keys), split_blocks(values), split_blocks(grad_attn), level_weight.reshape(N_CTX, TOK_DEV, H, LEVELS))

    def local_block(block_items):
        query3, key3, value3, grad3, weight_rows = block_items
        query_f = query3.astype(f32)
        key_f = key3.astype(f32)
        value_f = value3.astype(f32)
        grad_f = grad3.astype(f32)
        head_first = jnp.transpose(weight_rows, (1, 0, 2))
        weights = block_weights(head_first[:, :, :TOK_BITS + 1], level_map, causal, qk_scale)
        scores = (weights * jnp.einsum("phd,rhd->hpr", query_f, key_f)).astype(jnp.bfloat16)
        grad_scores = (weights * jnp.einsum("phd,rhd->hpr", grad_f, value_f)).astype(jnp.bfloat16)
        local_out = jnp.einsum("hpr,rhd->phd", scores.astype(f32), value_f)
        dq_local = jnp.einsum("hpr,rhd->phd", grad_scores.astype(f32), key_f)
        dk_local = jnp.einsum("hpr,phd->rhd", grad_scores.astype(f32), query_f)
        dv_local = jnp.einsum("hpr,phd->rhd", scores.astype(f32), grad_f)
        own_state = jnp.einsum("rhd,rhe->hde", key_f, value_f)
        far_weight = weight_rows[:, :, TOK_BITS + 1:]
        weighted = (jnp.transpose(far_weight, (2, 0, 1))[..., None] * query_f[None]).astype(jnp.bfloat16)
        adjoint_own = jnp.einsum("jphd,phe->jhde", weighted.astype(f32), grad_f)
        return local_out, dq_local, dk_local, dv_local, own_state, adjoint_own

    local_out, dq_local, dk_local, dv_local, own_states, adjoint_own = lax.map(local_block, items)

    seg_list = []
    adj_list = []
    for level_bit in range(CTX_BITS):
        span = 1 << level_bit
        grouped = own_states.reshape(N_CTX // (2 * span), 2, span, H, HD, HD)
        lower_sum = jnp.sum(grouped[:, 0], axis=1)
        has_bit = bit_table[:, level_bit][:, None, None, None]
        seg_list.append(jnp.repeat(lower_sum, 2 * span, axis=0) * has_bit)
        grouped_adj = adjoint_own[:, level_bit].reshape(N_CTX // (2 * span), 2, span, H, HD, HD)
        upper_sum = jnp.sum(grouped_adj[:, 1], axis=1)
        adj_list.append(jnp.repeat(upper_sum, 2 * span, axis=0) * (1.0 - has_bit))
    segments = jnp.stack(seg_list, 1)
    adjoints = jnp.stack(adj_list, 1)

    def far_block(block_items):
        query3, key3, value3, grad3, weight_rows, seg_state, adj_state, bit_set, near_out, near_dq, near_dk, near_dv = block_items
        query_f = query3.astype(f32)
        grad_f = grad3.astype(f32)
        far_set = weight_rows[:, :, TOK_BITS + 1:] * bit_set[None, None, :]
        through = jnp.einsum("phd,jhde->phje", query_f, seg_state, precision=high)
        far_out = jnp.einsum("phj,phje->phe", far_set, through, precision=high)
        attn = (near_out + qk_scale * far_out).astype(jnp.bfloat16)
        back_terms = jnp.einsum("phe,jhde->phjd", grad_f, seg_state, precision=high)
        dq_far = jnp.einsum("phj,phjd->phd", far_set, back_terms, precision=high)
        adj_masked = adj_state * (1.0 - bit_set)[:, None, None, None]
        dk_far = jnp.einsum("rhe,jhde->rhd", value3.astype(f32), adj_masked, precision=high)
        dv_far = jnp.einsum("rhd,jhde->rhe", key3.astype(f32), adj_masked, precision=high)
        grad_q = (near_dq + qk_scale * dq_far).astype(jnp.bfloat16)
        grad_k = (near_dk + qk_scale * dk_far).astype(jnp.bfloat16)
        grad_v = (near_dv + qk_scale * dv_far).astype(jnp.bfloat16)
        return attn, grad_q, grad_k, grad_v

    attn, grad_q, grad_k, grad_v = lax.map(far_block, items + (segments, adjoints, bit_table, local_out, dq_local, dk_local, dv_local))
    attn_out = attn.reshape(TOKENS, H * HD)
    group_cols = H // N_HEAD * HD
    layer_sum = jnp.zeros((TOKENS, D), f32)
    for group in range(N_HEAD):
        partial_out = jnp.dot(attn_out[:, group * group_cols:(group + 1) * group_cols], out_weight[group * group_cols:(group + 1) * group_cols], preferred_element_type=f32).astype(jnp.bfloat16)
        partial_out = lax.optimization_barrier(partial_out)
        layer_sum = layer_sum + partial_out.astype(f32)
    layer_out = layer_sum.astype(jnp.bfloat16)
    grad_weight = lax.dot_general(attn_out, cotangent, (((0,), (0,)), ((), ())), preferred_element_type=f32) * (TOKENS ** -0.5)
    return (layer_out, grad_q.reshape(TOKENS, H * HD), grad_k.reshape(TOKENS, H * HD), grad_v.reshape(TOKENS, H * HD), grad_weight)
```

```python
import jax
import jax.numpy as jnp
from jax import lax
from jax.sharding import PartitionSpec as P

HD = 128


def route(block, axis, pairs):
    return lax.ppermute(block, axis, pairs)


def swap(block, axis, flip):
    count = lax.axis_size(axis)
    return route(block, axis, [(i, i ^ flip) for i in range(count)])


def shift(block, step, groups, lowest, highest):
    pairs = []
    for group in range(max(lowest, 0), min(highest, groups - 1) + 1):
        if 0 <= group + step < groups:
            pairs += [(2 * group + side, 2 * (group + step) + side) for side in (0, 1)]
    return route(block, "ctx", pairs)


def level_scales(levels):
    level_ids = jnp.arange(levels, dtype=jnp.float32)
    return jnp.where(level_ids < 0.5, 1.0, jnp.exp2(-(level_ids - 1.0) * 0.5))


def token_levels(tok_rows, tok_bits):
    positions = jnp.arange(tok_rows, dtype=jnp.int32)
    xor_pos = jnp.bitwise_xor(positions[:, None], positions[None, :])
    level_map = jnp.zeros((tok_rows, tok_rows), jnp.int32)
    for step_bit in range(tok_bits):
        level_map = level_map + (xor_pos >= 1 << step_bit).astype(jnp.int32)
    return (level_map, positions[None, :] <= positions[:, None])


def block_weights(near_weight, level_map, causal, qk_scale):
    head_count, tok_rows, near_count = near_weight.shape
    running_sum = jnp.zeros((head_count, tok_rows, tok_rows), jnp.float32)
    for level_id in range(near_count):
        running_sum = running_sum + jnp.where(
            (level_map == level_id)[None], near_weight[:, :, level_id][:, :, None], 0.0
        )
    return jnp.where(causal[None], qk_scale * running_sum, 0.0)


def level_weights(level_table, table_index, level_column, levels):
    table_count, head_count, column_count = level_table.shape
    picked = (table_index[:, None] == jnp.arange(table_count, dtype=jnp.int32)[None, :]).astype(
        jnp.float32
    )
    columns = (
        level_column[:levels, None] == jnp.arange(column_count, dtype=jnp.int32)[None, :]
    ).astype(jnp.float32)
    by_level = jnp.einsum("nhc,lc->nhl", level_table, columns, precision=lax.Precision.HIGHEST)
    by_level = by_level * level_scales(levels)[None, None, :]
    per_token = jnp.einsum("tn,nhl->htl", picked, by_level, precision=lax.Precision.HIGHEST)
    return per_token


def body(queries, keys, values, cotangent, out_weight, level_table, table_index, level_column):
    f32 = jnp.float32
    bf16 = jnp.bfloat16
    tok_rows, feature_width = queries.shape
    head_count = feature_width // HD
    ctx_count = lax.axis_size("ctx")
    ctx_bits = ctx_count.bit_length() - 1
    tok_bits = tok_rows.bit_length() - 1
    levels = tok_bits + ctx_bits + 1
    qk_scale = HD ** (-0.5)
    ctx_index = lax.axis_index("ctx")
    head_index = lax.axis_index("head")
    heads = lax.axis_size("head")
    groups = ctx_count // 2
    side = ctx_index & 1
    group = ctx_index >> 1
    rows_h, wcols = out_weight.shape
    pieces = feature_width // wcols // 2

    cot4 = cotangent.reshape(tok_rows, pieces, 2, wcols)
    even, odd = cot4[:, :, 0].reshape(tok_rows, -1), cot4[:, :, 1].reshape(tok_rows, -1)
    kept = jnp.where(side == 0, even, odd)
    sent = jnp.where(side == 0, odd, even)
    cot_pair = jnp.concatenate([kept, swap(sent, "ctx", 1)], 0)[None]
    flip = heads // 2
    while flip:
        cot_pair = jnp.concatenate([cot_pair, swap(cot_pair, "head", flip)], 0)
        flip //= 2
    offsets = [0]
    flip = heads // 2
    while flip:
        offsets = offsets + [o ^ flip for o in offsets]
        flip //= 2
    slot_of = {o: i for i, o in enumerate(offsets)}

    def cot_chunk(chunk):
        relative = (chunk // pieces) ^ head_index
        slot = jnp.zeros((), jnp.int32)
        for o, i in slot_of.items():
            slot = jnp.where(relative == o, i, slot)
        part = lax.dynamic_index_in_dim(cot_pair, slot, 0, keepdims=False)
        return lax.dynamic_slice_in_dim(part, (chunk % pieces) * wcols, wcols, 1)

    def grad_part(chunk, weight):
        return lax.dot_general(
            cot_chunk(chunk), weight, (((1,), (1,)), ((), ())), preferred_element_type=f32
        )

    all_weight = jnp.zeros((groups + 1, rows_h, wcols), bf16)
    all_weight = lax.dynamic_update_index_in_dim(all_weight, out_weight, group, 0)
    grad_acc = grad_part(group, out_weight)
    rising = falling = out_weight
    for step in range(1, groups):
        rising = shift(rising, 1, groups, step - 1, groups)
        falling = shift(falling, -1, groups, 0, groups - step)
        if step < groups // 2:
            arrivals = [(rising, group >= step, group - step), (falling, group + step < groups, group + step)]
        else:
            below = group >= step
            arrivals = [
                (
                    rising + falling,
                    below | (group + step < groups),
                    jnp.where(below, group - step, group + step),
                )
            ]
        for chunk, valid, index in arrivals:
            grad_acc = grad_acc + grad_part(jnp.clip(index, 0, groups - 1), chunk)
            all_weight = lax.dynamic_update_index_in_dim(
                all_weight, chunk, jnp.where(valid, index, groups), 0
            )
    grad_theirs = swap(grad_acc[tok_rows:].astype(bf16), "ctx", 1)
    grad_attn = (grad_acc[:tok_rows] + grad_theirs.astype(f32)).astype(bf16)

    level_weight = level_weights(level_table, table_index, level_column, levels)
    level_map, causal = token_levels(tok_rows, tok_bits)
    weights = block_weights(level_weight[:, :, : tok_bits + 1], level_map, causal, qk_scale)
    far_weight = level_weight[:, :, tok_bits + 1 :]
    bit_set = jnp.stack([ctx_index >> level_bit & 1 for level_bit in range(ctx_bits)]).astype(f32)
    far_set = far_weight * bit_set[None, None, :] * qk_scale
    far_clear = (1.0 - bit_set) * qk_scale
    query3 = queries.reshape(tok_rows, head_count, HD)
    key3 = keys.reshape(tok_rows, head_count, HD)
    value3 = values.reshape(tok_rows, head_count, HD)
    own_state = jnp.einsum("rhd,rhe->hde", key3, value3, preferred_element_type=f32)
    running = own_state
    seg_list = []
    for step_bit in range(ctx_bits):
        partner_state = swap(running.astype(bf16), "ctx", 1 << step_bit)
        seg_list.append(partner_state)
        running = running + partner_state.astype(f32)
    products = jnp.einsum("phd,rhd->hpr", query3, key3, preferred_element_type=f32)
    scores = (weights * products).astype(bf16)
    out = jnp.einsum("hpr,rhd->phd", scores, value3, preferred_element_type=f32)
    for j in range(ctx_bits):
        through = jnp.einsum("phd,hde->phe", query3, seg_list[j], preferred_element_type=f32)
        out = out + far_set[:, :, j].T[:, :, None] * through
    attn_out = out.astype(bf16).reshape(tok_rows, feature_width)
    attn_pair = jnp.concatenate([attn_out, swap(attn_out, "ctx", 1)], 0)

    def weight_part(chunk):
        return lax.dot_general(
            attn_pair, cot_chunk(chunk), (((0,), (0,)), ((), ())), preferred_element_type=f32
        )

    up = down = None
    for step in range(1, groups):
        if step <= groups // 2:
            index = jnp.where(group < groups // 2, group + groups - step, group - groups + step)
            total = weight_part(jnp.clip(index, 0, groups - 1))
            if up is not None:
                total = total + up.astype(f32) + down.astype(f32)
            rise = fall = total.astype(bf16)
        else:
            rise = (weight_part(jnp.clip(group + groups - step, 0, groups - 1)) + up.astype(f32)).astype(bf16)
            fall = (weight_part(jnp.clip(group - groups + step, 0, groups - 1)) + down.astype(f32)).astype(bf16)
        up = shift(rise, 1, groups, 0, step - 1)
        down = shift(fall, -1, groups, groups - step, groups)
    tokens_all = tok_rows * ctx_count
    grad_weight = (weight_part(group) + up.astype(f32) + down.astype(f32)) * tokens_all ** (-0.5)

    def layer_part(offset):
        first = (head_index ^ offset) * pieces
        weight = lax.dynamic_slice_in_dim(all_weight, first, pieces, 0)
        return jnp.concatenate(
            [jnp.dot(attn_pair, weight[i], preferred_element_type=f32) for i in range(pieces)], 1
        )

    partials = {o: layer_part(o) for o in range(heads)}
    flip = 1
    while flip < heads:
        out_going = sorted(o for o in partials if o & flip)
        stacked = jnp.stack([partials[o].astype(bf16) for o in out_going], 0)
        came = swap(stacked, "head", flip)
        kept_parts = {}
        for i, o in enumerate(out_going):
            kept_parts[o ^ flip] = partials[o ^ flip] + came[i].astype(f32)
        partials = kept_parts
        flip *= 2
    layer = partials[0].astype(bf16)
    layer_own = layer[:tok_rows].reshape(tok_rows, pieces, wcols)
    layer_other = swap(layer[tok_rows:], "ctx", 1).reshape(tok_rows, pieces, wcols)
    layer_out = jnp.stack(
        [
            jnp.where(side == 0, layer_own, layer_other),
            jnp.where(side == 0, layer_other, layer_own),
        ],
        2,
    ).reshape(tok_rows, feature_width)

    grad3 = grad_attn.reshape(tok_rows, head_count, HD)
    query_h = jnp.transpose(query3, (1, 0, 2)).astype(f32)
    weighted = jnp.stack([(far_weight[:, :, j][:, :, None] * query_h).astype(bf16) for j in range(ctx_bits)], 0)
    pending = jnp.einsum("jhpd,phe->jhde", weighted, grad3, preferred_element_type=f32)
    adjoint = jnp.zeros((head_count, HD, HD), f32)
    for step_bit in range(ctx_bits):
        partner = swap(pending.astype(bf16), "ctx", 1 << step_bit).astype(f32)
        adjoint = adjoint + far_clear[step_bit] * partner[0]
        pending = (pending + partner)[1:]
    adjoint = adjoint.astype(bf16)
    grad_products = jnp.einsum("phd,rhd->hpr", grad3, value3, preferred_element_type=f32)
    grad_scores = (weights * grad_products).astype(bf16)
    dq = jnp.einsum("hpr,rhd->phd", grad_scores, key3, preferred_element_type=f32)
    dk = jnp.einsum("hpr,phd->rhd", grad_scores, query3, preferred_element_type=f32)
    dv = jnp.einsum("hpr,phd->rhd", scores, grad3, preferred_element_type=f32)
    for j in range(ctx_bits):
        back = jnp.einsum("phe,hde->phd", grad3, seg_list[j], preferred_element_type=f32)
        dq = dq + far_set[:, :, j].T[:, :, None] * back
    dk = dk + jnp.einsum("rhe,hde->rhd", value3, adjoint, preferred_element_type=f32)
    dv = dv + jnp.einsum("rhd,hde->rhe", key3, adjoint, preferred_element_type=f32)
    grad_queries = dq.astype(bf16).reshape(tok_rows, feature_width)
    grad_keys = dk.astype(bf16).reshape(tok_rows, feature_width)
    grad_values = dv.astype(bf16).reshape(tok_rows, feature_width)
    return (layer_out, grad_queries, grad_keys, grad_values, grad_weight)


def solution(mesh):
    placed = (
        P("ctx", "head"),
        P("ctx", "head"),
        P("ctx", "head"),
        P("ctx", "head"),
        P("head", "ctx"),
        P(None, "head", None),
        P("ctx"),
        P(),
    )
    return jax.shard_map(
        body,
        mesh=mesh,
        in_specs=placed,
        out_specs=(
            P("ctx", "head"),
            P("ctx", "head"),
            P("ctx", "head"),
            P("ctx", "head"),
            P("head", "ctx"),
        ),
        check_vma=False,
    )
```

```python
import functools

import jax
import jax.numpy as jnp
from jax import lax
from jax.experimental import pallas as pl
from jax.sharding import PartitionSpec as P

HD = 128
F32 = jnp.float32
BF16 = jnp.bfloat16


def route(block, axis, pairs):
    return lax.ppermute(block, axis, pairs)


def swap(block, axis, flip):
    count = lax.axis_size(axis)
    return route(block, axis, [(i, i ^ flip) for i in range(count)])


def shift(block, step, groups, lowest, highest):
    pairs = []
    for group in range(max(lowest, 0), min(highest, groups - 1) + 1):
        if 0 <= group + step < groups:
            pairs += [(2 * group + side, 2 * (group + step) + side) for side in (0, 1)]
    return route(block, "ctx", pairs)


def dot_nn(a, b):
    return lax.dot_general(a, b, (((1,), (0,)), ((), ())), preferred_element_type=F32)


def dot_nt(a, b):
    return lax.dot_general(a, b, (((1,), (1,)), ((), ())), preferred_element_type=F32)


def dot_tn(a, b):
    return lax.dot_general(a, b, (((0,), (0,)), ((), ())), preferred_element_type=F32)


def halves(x):
    high = lax.reduce_precision(x, 8, 7)
    return high.astype(BF16), (x - high).astype(BF16)


def near_blocks(tok_rows):
    blocks = [(at, at, HD, None) for at in range(0, tok_rows, HD)]
    size = HD
    while size < tok_rows:
        level = size.bit_length()
        blocks += [(at + size, at, size, level) for at in range(0, tok_rows, 2 * size)]
        size *= 2
    return blocks


def diagonal(lam_of, causal, bits):
    weight = lam_of(0)
    for level in range(1, HD.bit_length()):
        weight = jnp.where(bits >= 1 << level - 1, lam_of(level), weight)
    return jnp.where(causal, weight, 0.0)


def masks():
    row = lax.broadcasted_iota(jnp.int32, (HD, HD), 0)
    col = lax.broadcasted_iota(jnp.int32, (HD, HD), 1)
    return row, col, row ^ col


def weight_rows(lam, row, size, level, where):
    part = lam[row : row + size]
    if level is not None:
        return part[:, level : level + 1]
    r, c, bits = where
    return diagonal(lambda l: part[:, l : l + 1], c <= r, bits)


def weight_cols(lam_t, row, size, level, where):
    part = lam_t[:, row : row + size]
    if level is not None:
        return part[level : level + 1]
    r, c, bits = where
    return diagonal(lambda l: part[l : l + 1], r <= c, bits)


def add_rows(total, at, part):
    for i in range(0, part.shape[0], HD):
        slot = (at + i) // HD
        piece = part[i : i + HD]
        total[slot] = piece if total[slot] is None else total[slot] + piece


def state_kernel(pack, k_ref, v_ref, o_ref):
    for n in range(pack):
        at = pl.ds(n * HD, HD)
        o_ref[n] = dot_tn(k_ref[:, at], v_ref[:, at])


def forward_kernel(pack, far, levels, q_ref, k_ref, v_ref, picked_ref, table_ref, *refs):
    segs, o_ref = refs[:far], refs[far]
    tok_rows = q_ref.shape[0]
    where = masks()
    for n in range(pack):
        q, k, v = (ref[:, pl.ds(n * HD, HD)] for ref in (q_ref, k_ref, v_ref))
        lam = dot_nn(picked_ref[...], table_ref[n])
        total = [None] * (tok_rows // HD)
        for row, col, size, level in near_blocks(tok_rows):
            weight = weight_rows(lam, row, size, level, where)
            score = dot_nt(q[row : row + size], k[col : col + size])
            add_rows(total, row, dot_nn((weight * score).astype(BF16), v[col : col + size]))
        through = dot_nn(q, jnp.concatenate([seg[n] for seg in segs], 1))
        for i in range(tok_rows // HD):
            out = total[i]
            at = i * HD
            for j in range(far):
                scale = lam[at : at + HD, levels + j : levels + j + 1]
                out = out + scale * through[at : at + HD, j * HD : (j + 1) * HD]
            o_ref[at : at + HD, pl.ds(n * HD, HD)] = out.astype(BF16)


def adjoint_kernel(pack, far, near, q_ref, g_ref, picked_ref, table_ref, o_ref):
    for n in range(pack):
        lam = dot_nn(table_ref[n], picked_ref[...])
        q_t = q_ref[:, pl.ds(n * HD, HD)].T.astype(F32)
        stacked = jnp.concatenate(
            [(lam[near + j : near + j + 1] * q_t).astype(BF16) for j in range(far)], 0
        )
        found = dot_nn(stacked, g_ref[:, pl.ds(n * HD, HD)])
        for j in range(far):
            o_ref[j, n] = found[j * HD : (j + 1) * HD]


def backward_kernel(
    pack, far, levels, q_ref, k_ref, v_ref, g_ref, column_ref, row_ref, table_ref, flipped_ref, *refs
):
    segs, (dq_ref, dk_ref, dv_ref) = refs[:far], refs[far:]
    tok_rows = q_ref.shape[0]
    where = masks()
    for n in range(pack):
        lanes = pl.ds(n * HD, HD)
        q_all, k_all, v_all, g_all = (ref[:, lanes] for ref in (q_ref, k_ref, v_ref, g_ref))
        lam = dot_nn(column_ref[...], table_ref[n])
        lam_t = dot_nn(flipped_ref[n], row_ref[...])
        dq, dk, dv = ([None] * (tok_rows // HD) for _ in range(3))
        for row, col, size, level in near_blocks(tok_rows):
            q, g = q_all[row : row + size], g_all[row : row + size]
            k, v = k_all[col : col + size], v_all[col : col + size]
            weight = weight_rows(lam, row, size, level, where)
            flipped = weight_cols(lam_t, row, size, level, where)
            add_rows(dq, row, dot_nn((weight * dot_nt(g, v)).astype(BF16), k))
            add_rows(dk, col, dot_nn((flipped * dot_nt(v, g)).astype(BF16), q))
            add_rows(dv, col, dot_nn((flipped * dot_nt(k, q)).astype(BF16), g))
        back = dot_nt(g_all, jnp.concatenate([seg[n] for seg in segs], 0))
        for i in range(tok_rows // HD):
            out = dq[i]
            at = i * HD
            for j in range(far):
                scale = lam[at : at + HD, levels + j : levels + j + 1]
                out = out + scale * back[at : at + HD, j * HD : (j + 1) * HD]
            dq_ref[at : at + HD, lanes] = out.astype(BF16)
            dk_ref[at : at + HD, lanes] = dk[i]
            dv_ref[at : at + HD, lanes] = dv[i]


def finish_kernel(pack, k_ref, v_ref, dk_ref, dv_ref, a_ref, dk_out, dv_out):
    for n in range(pack):
        lanes = pl.ds(n * HD, HD)
        adjoint = a_ref[n]
        dk_out[:, lanes] = (dk_ref[:, lanes] + dot_nt(v_ref[:, lanes], adjoint)).astype(BF16)
        dv_out[:, lanes] = (dv_ref[:, lanes] + dot_nn(k_ref[:, lanes], adjoint)).astype(BF16)


def shape(dims, kind):
    return jax.ShapeDtypeStruct(dims, kind)


def per_head(name, kernel, most, flops, ins, outs, consts=()):
    width = ins[0].shape[1]
    heads = width // HD
    pack = min(most, heads)

    def spec(x):
        if len(x.shape) == 2:
            return pl.BlockSpec((x.shape[0], pack * HD), lambda h: (0, h))
        lead = (0,) * (len(x.shape) - 3)
        return pl.BlockSpec(x.shape[:-3] + (pack,) + x.shape[-2:], lambda h: lead + (h, 0, 0))

    size = sum(x.size * x.dtype.itemsize for x in tuple(ins) + tuple(outs))
    whole = [pl.BlockSpec(x.shape, lambda h: (0, 0)) for x in consts]
    single = len(outs) == 1
    return pl.pallas_call(
        functools.partial(kernel, pack),
        grid=(heads // pack,),
        in_specs=whole + [spec(x) for x in ins],
        out_specs=spec(outs[0]) if single else [spec(x) for x in outs],
        out_shape=outs[0] if single else list(outs),
        name=name,
        cost_estimate=pl.CostEstimate(flops=flops, bytes_accessed=size, transcendentals=0),
    )(*consts, *ins)


def states_of(keys, values, pack=4):
    rows, width = keys.shape
    heads = width // HD
    return per_head(
        "states", state_kernel, pack, 2 * rows * width * HD, (keys, values), (shape((heads, HD, HD), F32),)
    )


def forward_of(queries, keys, values, column, table, segs, levels, pack=2):
    rows, width = queries.shape

    def kernel(pack, picked, *refs):
        forward_kernel(pack, len(segs), levels, *refs[:3], picked, *refs[3:])

    return per_head(
        "attend", kernel, pack, 6 * rows * rows * width,
        (queries, keys, values, table, *segs), (shape((rows, width), BF16),), (column,),
    )


def adjoints_of(queries, grad, row, flipped, near, far, pack=4):
    rows, width = queries.shape

    def kernel(pack, picked, q, g, table, out):
        adjoint_kernel(pack, far, near, q, g, picked, table, out)

    return per_head(
        "adjoints", kernel, pack, 2 * far * rows * width * HD,
        (queries, grad, flipped), (shape((far, width // HD, HD, HD), F32),), (row,),
    )


def backward_of(queries, keys, values, grad, column, row, table, flipped, segs, levels, pack=2):
    rows, width = queries.shape

    def kernel(pack, column, row, *refs):
        backward_kernel(pack, len(segs), levels, *refs[:4], column, row, *refs[4:])

    return per_head(
        "retreat", kernel, pack, 12 * rows * rows * width,
        (queries, keys, values, grad, table, flipped, *segs),
        (shape((rows, width), BF16), shape((rows, width), F32), shape((rows, width), F32)),
        (column, row),
    )


def finish_of(keys, values, dk, dv, adjoint, pack=4):
    rows, width = keys.shape
    return per_head(
        "finish", finish_kernel, pack, 4 * rows * width * HD,
        (keys, values, dk, dv, adjoint), (shape((rows, width), BF16),) * 2,
    )


def level_scales(levels):
    level_ids = jnp.arange(levels, dtype=jnp.float32)
    return jnp.where(level_ids < 0.5, 1.0, jnp.exp2(-(level_ids - 1.0) * 0.5))


def level_tables(level_table, level_column, levels, near, ctx_bits, ctx_index):
    columns = (
        level_column[:levels, None] == jnp.arange(level_table.shape[2], dtype=jnp.int32)[None, :]
    ).astype(F32)
    scaled = columns * (level_scales(levels) * HD ** (-0.5))[:, None]
    bits = (ctx_index >> jnp.arange(ctx_bits, dtype=jnp.int32) & 1).astype(F32)
    scaled = jnp.concatenate([scaled, scaled[near:] * bits[:, None]], 0)
    table = jnp.sum(level_table.transpose(1, 0, 2)[:, :, None, :] * scaled[None, None], -1)
    high, low = halves(table)
    return jnp.concatenate([high, low], 1)


def picked_rows(table_index, table_count):
    ids = jnp.arange(2 * table_count, dtype=jnp.int32) % table_count
    column = (table_index[:, None] == ids[None, :]).astype(BF16)
    row = (table_index[None, :] == ids[:, None]).astype(BF16)
    return column, row


def body(queries, keys, values, cotangent, out_weight, level_table, table_index, level_column):
    f32 = jnp.float32
    bf16 = jnp.bfloat16
    tok_rows, feature_width = queries.shape
    ctx_count = lax.axis_size("ctx")
    ctx_bits = ctx_count.bit_length() - 1
    tok_bits = tok_rows.bit_length() - 1
    levels = tok_bits + ctx_bits + 1
    ctx_index = lax.axis_index("ctx")
    head_index = lax.axis_index("head")
    heads = lax.axis_size("head")
    groups = ctx_count // 2
    side = ctx_index & 1
    group = ctx_index >> 1
    rows_h, wcols = out_weight.shape
    pieces = feature_width // wcols // 2

    cot4 = cotangent.reshape(tok_rows, pieces, 2, wcols)
    even, odd = cot4[:, :, 0].reshape(tok_rows, -1), cot4[:, :, 1].reshape(tok_rows, -1)
    kept = jnp.where(side == 0, even, odd)
    sent = jnp.where(side == 0, odd, even)
    cot_pair = jnp.concatenate([kept, swap(sent, "ctx", 1)], 0)[None]
    flip = heads // 2
    while flip:
        cot_pair = jnp.concatenate([cot_pair, swap(cot_pair, "head", flip)], 0)
        flip //= 2
    offsets = [0]
    flip = heads // 2
    while flip:
        offsets = offsets + [o ^ flip for o in offsets]
        flip //= 2
    slot_of = {o: i for i, o in enumerate(offsets)}

    def cot_chunk(chunk):
        relative = (chunk // pieces) ^ head_index
        slot = jnp.zeros((), jnp.int32)
        for o, i in slot_of.items():
            slot = jnp.where(relative == o, i, slot)
        part = lax.dynamic_index_in_dim(cot_pair, slot, 0, keepdims=False)
        return lax.dynamic_slice_in_dim(part, (chunk % pieces) * wcols, wcols, 1)

    def grad_part(chunk, weight):
        return lax.dot_general(
            cot_chunk(chunk), weight, (((1,), (1,)), ((), ())), preferred_element_type=f32
        )

    all_weight = jnp.zeros((groups + 1, rows_h, wcols), bf16)
    all_weight = lax.dynamic_update_index_in_dim(all_weight, out_weight, group, 0)
    grad_acc = grad_part(group, out_weight)
    rising = falling = out_weight
    for step in range(1, groups):
        rising = shift(rising, 1, groups, step - 1, groups)
        falling = shift(falling, -1, groups, 0, groups - step)
        if step < groups // 2:
            arrivals = [(rising, group >= step, group - step), (falling, group + step < groups, group + step)]
        else:
            below = group >= step
            arrivals = [
                (
                    rising + falling,
                    below | (group + step < groups),
                    jnp.where(below, group - step, group + step),
                )
            ]
        for chunk, valid, index in arrivals:
            grad_acc = grad_acc + grad_part(jnp.clip(index, 0, groups - 1), chunk)
            all_weight = lax.dynamic_update_index_in_dim(
                all_weight, chunk, jnp.where(valid, index, groups), 0
            )
    grad_theirs = swap(grad_acc[tok_rows:].astype(bf16), "ctx", 1)
    grad_attn = (grad_acc[:tok_rows] + grad_theirs.astype(f32)).astype(bf16)

    column, row = picked_rows(table_index, level_table.shape[0])
    table = level_tables(level_table, level_column, levels, tok_bits + 1, ctx_bits, ctx_index)
    flipped = table.transpose(0, 2, 1)
    running = states_of(keys, values)
    seg_list = []
    for step_bit in range(ctx_bits):
        with jax.named_scope(f"seg{step_bit}"):
            partner_state = swap(running.astype(bf16), "ctx", 1 << step_bit)
        seg_list.append(partner_state)
        running = running + partner_state.astype(f32)
    attn_out = forward_of(queries, keys, values, column, table, seg_list, levels)
    attn_pair = jnp.concatenate([attn_out, swap(attn_out, "ctx", 1)], 0)

    def weight_part(chunk):
        return lax.dot_general(
            attn_pair, cot_chunk(chunk), (((0,), (0,)), ((), ())), preferred_element_type=f32
        )

    up = down = None
    for step in range(1, groups):
        if step <= groups // 2:
            index = jnp.where(group < groups // 2, group + groups - step, group - groups + step)
            total = weight_part(jnp.clip(index, 0, groups - 1))
            if up is not None:
                total = total + up.astype(f32) + down.astype(f32)
            rise = fall = total.astype(bf16)
        else:
            rise = (weight_part(jnp.clip(group + groups - step, 0, groups - 1)) + up.astype(f32)).astype(bf16)
            fall = (weight_part(jnp.clip(group - groups + step, 0, groups - 1)) + down.astype(f32)).astype(bf16)
        up = shift(rise, 1, groups, 0, step - 1)
        down = shift(fall, -1, groups, groups - step, groups)
    tokens_all = tok_rows * ctx_count
    grad_weight = (weight_part(group) + up.astype(f32) + down.astype(f32)) * tokens_all ** (-0.5)

    def layer_part(offset):
        first = (head_index ^ offset) * pieces
        weight = lax.dynamic_slice_in_dim(all_weight, first, pieces, 0)
        return jnp.concatenate(
            [jnp.dot(attn_pair, weight[i], preferred_element_type=f32) for i in range(pieces)], 1
        )

    partials = {o: layer_part(o) for o in range(heads)}
    flip = 1
    while flip < heads:
        out_going = sorted(o for o in partials if o & flip)
        stacked = jnp.stack([partials[o].astype(bf16) for o in out_going], 0)
        came = swap(stacked, "head", flip)
        kept_parts = {}
        for i, o in enumerate(out_going):
            kept_parts[o ^ flip] = partials[o ^ flip] + came[i].astype(f32)
        partials = kept_parts
        flip *= 2
    layer = partials[0].astype(bf16)
    layer_own = layer[:tok_rows].reshape(tok_rows, pieces, wcols)
    layer_other = swap(layer[tok_rows:], "ctx", 1).reshape(tok_rows, pieces, wcols)
    layer_out = jnp.stack(
        [
            jnp.where(side == 0, layer_own, layer_other),
            jnp.where(side == 0, layer_other, layer_own),
        ],
        2,
    ).reshape(tok_rows, feature_width)

    far_clear = (1 - (ctx_index >> jnp.arange(ctx_bits) & 1)).astype(f32)
    pending = adjoints_of(queries, grad_attn, row, flipped, tok_bits + 1, ctx_bits)
    adjoint = jnp.zeros(pending.shape[1:], f32)
    for step_bit in range(ctx_bits):
        with jax.named_scope(f"adj{step_bit}"):
            partner = swap(pending.astype(bf16), "ctx", 1 << step_bit).astype(f32)
        adjoint = adjoint + far_clear[step_bit] * partner[0]
        pending = (pending + partner)[1:]
    grad_queries, near_dk, near_dv = backward_of(
        queries, keys, values, grad_attn, column, row, table, flipped, seg_list, levels
    )
    grad_keys, grad_values = finish_of(keys, values, near_dk, near_dv, adjoint.astype(bf16))
    return (layer_out, grad_queries, grad_keys, grad_values, grad_weight)


def solution(mesh):
    placed = (
        P("ctx", "head"),
        P("ctx", "head"),
        P("ctx", "head"),
        P("ctx", "head"),
        P("head", "ctx"),
        P(None, "head", None),
        P("ctx"),
        P(),
    )
    return jax.shard_map(
        body,
        mesh=mesh,
        in_specs=placed,
        out_specs=(
            P("ctx", "head"),
            P("ctx", "head"),
            P("ctx", "head"),
            P("ctx", "head"),
            P("head", "ctx"),
        ),
        check_vma=False,
    )
```

```python
import jax
import jax.numpy as jnp
from jax import lax
from jax.experimental import pallas as pl
from jax.experimental.pallas import tpu as pltpu
from jax.sharding import PartitionSpec as P


HD = 128
F32 = jnp.float32
BF16 = jnp.bfloat16


def route(block, axis, pairs):
    return lax.ppermute(block, axis, pairs)


def swap(block, axis, flip, upward=False, downward=False):
    pairs = [(i, i ^ flip) for i in range(lax.axis_size(axis))]
    if upward:
        pairs = [(i, j) for i, j in pairs if i < j]
    if downward:
        pairs = [(i, j) for i, j in pairs if i > j]
    return route(block, axis, pairs)


def shift(block, groups, up=None, down=None):
    pairs = []
    for step, reach in ((1, up), (-1, down)):
        if reach is None:
            continue
        for group in range(max(reach[0], 0), min(reach[1], groups - 1) + 1):
            if 0 <= group + step < groups:
                pairs += [(2 * group + side, 2 * (group + step) + side) for side in (0, 1)]
    return route(block, "ctx", pairs)


def dot_nn(a, b):
    return lax.dot_general(a, b, (((1,), (0,)), ((), ())), preferred_element_type=F32)


def dot_nt(a, b):
    return lax.dot_general(a, b, (((1,), (1,)), ((), ())), preferred_element_type=F32)


def dot_tn(a, b):
    return lax.dot_general(a, b, (((0,), (0,)), ((), ())), preferred_element_type=F32)


def halves(x):
    high = lax.reduce_precision(x, 8, 7)
    return high.astype(BF16), (x - high).astype(BF16)


def near_blocks(tok_rows):
    blocks = [(at, at, HD, None) for at in range(0, tok_rows, HD)]
    size = HD
    while size < tok_rows:
        level = size.bit_length()
        blocks += [(at + size, at, size, level) for at in range(0, tok_rows, 2 * size)]
        size *= 2
    return blocks


def masks():
    row = lax.broadcasted_iota(jnp.int32, (HD, HD), 0)
    col = lax.broadcasted_iota(jnp.int32, (HD, HD), 1)
    level = jnp.zeros((HD, HD), jnp.int32)
    for bit in range(HD.bit_length() - 1):
        level = level + ((row ^ col) >= 1 << bit).astype(jnp.int32)
    return jnp.where(col <= row, level, HD - 1), level, row <= col


def weight_rows(lam, row, size, level, where):
    part = lam[row : row + size]
    if level is not None:
        return part[:, level : level + 1]
    return jnp.take_along_axis(part, where[0], axis=1, mode="promise_in_bounds")


def weight_cols(lam_t, row, size, level, where):
    part = lam_t[:, row : row + size]
    if level is not None:
        return part[level : level + 1]
    rows = [
        jnp.take_along_axis(part[:8], where[1][i : i + 8], axis=0, mode="promise_in_bounds")
        for i in range(0, HD, 8)
    ]
    return jnp.where(where[2], jnp.concatenate(rows, 0), 0.0)


def add_rows(total, at, part):
    for i in range(0, part.shape[0], HD):
        slot = (at + i) // HD
        piece = part[i : i + HD]
        total[slot] = piece if total[slot] is None else total[slot] + piece


def state_kernel(pack, k_ref, v_ref, o_ref):
    for n in range(pack):
        at = pl.ds(n * HD, HD)
        o_ref[n] = dot_tn(k_ref[:, at], v_ref[:, at]).astype(BF16)


def near_kernel(pack, q_ref, k_ref, v_ref, picked_ref, table_ref, o_ref):
    tok_rows = q_ref.shape[0]
    where = masks()
    for n in range(pack):
        q, k, v = (ref[:, pl.ds(n * HD, HD)] for ref in (q_ref, k_ref, v_ref))
        lam = dot_nn(picked_ref[...], table_ref[n])
        total = [None] * (tok_rows // HD)
        for row, col, size, level in near_blocks(tok_rows):
            weight = weight_rows(lam, row, size, level, where)
            score = dot_nt(q[row : row + size], k[col : col + size])
            add_rows(total, row, dot_nn((weight * score).astype(BF16), v[col : col + size]))
        for i in range(tok_rows // HD):
            o_ref[i * HD : (i + 1) * HD, pl.ds(n * HD, HD)] = total[i]


def far_kernel(pack, far, levels, near_ref, q_ref, picked_ref, table_ref, *refs):
    segs, o_ref = refs[:far], refs[far]
    for n in range(pack):
        lanes = pl.ds(n * HD, HD)
        lam = dot_nn(picked_ref[...], table_ref[n])
        through = dot_nn(q_ref[:, lanes], jnp.concatenate([seg[n] for seg in segs], 1))
        out = near_ref[:, lanes]
        for j in range(far):
            out = out + lam[:, levels + j : levels + j + 1] * through[:, j * HD : (j + 1) * HD]
        o_ref[:, lanes] = out.astype(BF16)


def adjoint_kernel(pack, far, near, picked_ref, q_ref, mine_ref, theirs_ref, table_ref, o_ref, g_ref):
    for n in range(pack):
        lanes = pl.ds(n * HD, HD)
        g = (mine_ref[:, lanes] + theirs_ref[:, lanes].astype(F32)).astype(BF16)
        g_ref[:, lanes] = g
        lam = dot_nn(table_ref[n], picked_ref[...])
        q_t = q_ref[:, lanes].T.astype(F32)
        stacked = jnp.concatenate(
            [(lam[near + j : near + j + 1] * q_t).astype(BF16) for j in range(far)], 0
        )
        found = dot_nn(stacked, g)
        for j in range(far):
            o_ref[j, n] = found[j * HD : (j + 1) * HD].astype(BF16)


def backward_kernel(
    pack, far, levels, q_ref, k_ref, v_ref, g_ref, column_ref, row_ref, table_ref, flipped_ref, *refs
):
    segs, (dq_ref, dk_ref, dv_ref) = refs[:far], refs[far:]
    tok_rows = q_ref.shape[0]
    where = masks()
    for n in range(pack):
        lanes = pl.ds(n * HD, HD)
        q_all, k_all, v_all, g_all = (ref[:, lanes] for ref in (q_ref, k_ref, v_ref, g_ref))
        lam = dot_nn(column_ref[...], table_ref[n])
        lam_t = dot_nn(flipped_ref[n], row_ref[...])
        dq, dk, dv = ([None] * (tok_rows // HD) for _ in range(3))
        for row, col, size, level in near_blocks(tok_rows):
            q, g = q_all[row : row + size], g_all[row : row + size]
            k, v = k_all[col : col + size], v_all[col : col + size]
            weight = weight_rows(lam, row, size, level, where)
            flipped = weight_cols(lam_t, row, size, level, where)
            add_rows(dq, row, dot_nn((weight * dot_nt(g, v)).astype(BF16), k))
            add_rows(dk, col, dot_nn((flipped * dot_nt(v, g)).astype(BF16), q))
            add_rows(dv, col, dot_nn((flipped * dot_nt(k, q)).astype(BF16), g))
        back = dot_nt(g_all, jnp.concatenate([seg[n] for seg in segs], 0))
        for i in range(tok_rows // HD):
            out = dq[i]
            at = i * HD
            for j in range(far):
                scale = lam[at : at + HD, levels + j : levels + j + 1]
                out = out + scale * back[at : at + HD, j * HD : (j + 1) * HD]
            dq_ref[at : at + HD, lanes] = out.astype(BF16)
            dk_ref[at : at + HD, lanes] = dk[i]
            dv_ref[at : at + HD, lanes] = dv[i]


def finish_kernel(pack, far, clear_ref, k_ref, v_ref, dk_ref, dv_ref, *refs):
    found, (dk_out, dv_out) = refs[:far], refs[far:]
    for n in range(pack):
        lanes = pl.ds(n * HD, HD)
        adjoint = clear_ref[0:1] * found[0][0, n].astype(F32)
        for j in range(1, far):
            adjoint = adjoint + clear_ref[j : j + 1] * found[j][0, n].astype(F32)
        adjoint = adjoint.astype(BF16)
        dk_out[:, lanes] = (dk_ref[:, lanes] + dot_nt(v_ref[:, lanes], adjoint)).astype(BF16)
        dv_out[:, lanes] = (dv_ref[:, lanes] + dot_nn(k_ref[:, lanes], adjoint)).astype(BF16)


def shape(dims, kind):
    return jax.ShapeDtypeStruct(dims, kind)


def per_head(kernel, most, flops, heads, first, ins, outs, consts=(), into=()):
    pack = min(most, heads)

    def spec(x):
        if len(x.shape) == 2:
            at = first // pack if x.shape[1] > heads * HD else 0
            return pl.BlockSpec((x.shape[0], pack * HD), lambda h: (0, h + at))
        at = first // pack if x.shape[-3] > heads else 0
        lead = (0,) * (len(x.shape) - 3)
        return pl.BlockSpec(x.shape[:-3] + (pack,) + x.shape[-2:], lambda h: lead + (h + at, 0, 0))

    def run(*refs):
        kernel(pack, *refs[len(into) :])

    size = flops // HD + sum(x.size * x.dtype.itemsize for x in outs)
    whole = [pl.BlockSpec(x.shape, lambda h: (0, 0)) for x in consts]
    kept = [pl.BlockSpec(memory_space=pl.ANY)] * len(into)
    single = len(outs) == 1
    return pl.pallas_call(
        run,
        grid=(heads // pack,),
        in_specs=kept + whole + [spec(x) for x in ins],
        out_specs=spec(outs[0]) if single else [spec(x) for x in outs],
        out_shape=outs[0] if single else list(outs),
        input_output_aliases={i: i for i in range(len(into))},
        cost_estimate=pl.CostEstimate(flops=flops, bytes_accessed=size, transcendentals=0),
    )(*into, *consts, *ins)


def states_of(keys, values):
    rows, width = keys.shape
    heads = width // HD
    return per_head(
        state_kernel, 4, 2 * rows * width * HD, heads, 0,
        (keys, values), (shape((heads, HD, HD), BF16),),
    )


def near_of(queries, keys, values, column, table):
    rows, width = queries.shape

    def kernel(pack, picked, q, k, v, table, out):
        near_kernel(pack, q, k, v, picked, table, out)

    return per_head(
        kernel, 2, 6 * rows * rows * width, width // HD, 0,
        (queries, keys, values, table), (shape((rows, width), F32),), (column,),
    )


def far_of(near, queries, column, table, segs, levels, heads, first):
    rows = queries.shape[0]

    def kernel(pack, picked, *refs):
        far_kernel(pack, len(segs), levels, *refs[:2], picked, *refs[2:])

    return per_head(
        kernel, 2, 2 * len(segs) * rows * heads * HD * HD, heads, first,
        (near, queries, table, *segs), (shape((rows, heads * HD), BF16),), (column,),
    )


def adjoints_of(queries, mine, theirs, row, flipped, near, far, heads, first):
    rows = queries.shape[0]

    def kernel(pack, *refs):
        adjoint_kernel(pack, far, near, *refs)

    return per_head(
        kernel, 4, 2 * far * rows * heads * HD * HD, heads, first,
        (queries, mine, theirs, flipped),
        (shape((far, heads, HD, HD), BF16), shape((rows, heads * HD), BF16)), (row,),
    )


def backward_of(queries, keys, values, grad, column, row, table, flipped, segs, levels, heads, first, into):
    rows, width = queries.shape

    def kernel(pack, column, row, *refs):
        backward_kernel(pack, len(segs), levels, *refs[:4], column, row, *refs[4:])

    part = shape((rows, heads * HD), F32)
    return per_head(
        kernel, 2, 12 * rows * rows * heads * HD, heads, first,
        (queries, keys, values, grad, table, flipped, *segs),
        (shape((rows, width), BF16), part, part), (column, row), into,
    )


def finish_of(keys, values, dk, dv, found, clear, heads, first, into):
    rows, width = keys.shape

    def kernel(pack, *refs):
        finish_kernel(pack, len(found), *refs)

    return per_head(
        kernel, 4, 4 * rows * heads * HD * HD, heads, first,
        (keys, values, dk, dv, *found), (shape((rows, width), BF16),) * 2, (clear,), into,
    )


def layer_kernel(sources, adds, tile, chosen_ref, mine_ref, theirs_ref, *refs):
    weights, came, o_ref, held = refs[:sources], refs[sources:-2], refs[-2], refs[-1]
    here = chosen_ref[pl.program_id(0)]
    for i in range(sources):

        @pl.when(here == i)
        def _(i=i):
            held[...] = weights[i][...]

    rows = mine_ref.shape[0]
    for k, ref in enumerate((mine_ref, theirs_ref)):

        @pl.loop(0, rows // tile)
        def _(t, k=k, ref=ref):
            at = pl.multiple_of(t * tile, tile)
            total = dot_nn(ref[pl.ds(at, tile)], held[...])
            if adds:
                total = total + came[0][0, pl.ds(k * rows + at, tile)].astype(F32)
            o_ref[0, pl.ds(k * rows + at, tile)] = total.astype(BF16)


def layer_of(chosen, mine, theirs, weights, came=None):
    rows, width = mine.shape
    count, cols = chosen.shape[0], weights[0].shape[1]
    whole = lambda x: pl.BlockSpec(x.shape, lambda j, c: (0, 0), pipeline_mode=pl.Buffered(1))
    piece = pl.BlockSpec((1, 2 * rows, cols), lambda j, c: (j, 0, 0))
    adds = () if came is None else (came,)

    def kernel(*refs):
        layer_kernel(len(weights), len(adds), min(256, rows), *refs)

    return pl.pallas_call(
        kernel,
        grid_spec=pltpu.PrefetchScalarGridSpec(
            num_scalar_prefetch=1,
            grid=(count,),
            in_specs=[whole(x) for x in (mine, theirs, *weights)] + [piece] * len(adds),
            out_specs=piece,
            scratch_shapes=[pltpu.VMEM(weights[0].shape, BF16)],
        ),
        out_shape=shape((count, 2 * rows, cols), BF16),
        name="layer",
        cost_estimate=pl.CostEstimate(
            flops=4 * count * rows * width * cols, bytes_accessed=4 * count * rows * cols, transcendentals=0
        ),
    )(chosen, mine, theirs, *weights, *adds)


def level_scales(levels):
    level_ids = jnp.arange(levels, dtype=jnp.float32)
    return jnp.where(level_ids < 0.5, 1.0, jnp.exp2(-(level_ids - 1.0) * 0.5))


def level_tables(level_table, level_column, levels, near, ctx_bits, ctx_index):
    columns = (
        level_column[:levels, None] == jnp.arange(level_table.shape[2], dtype=jnp.int32)[None, :]
    ).astype(F32)
    scaled = columns * (level_scales(levels) * HD ** (-0.5))[:, None]
    bits = (ctx_index >> jnp.arange(ctx_bits, dtype=jnp.int32) & 1).astype(F32)
    scaled = jnp.concatenate([scaled, scaled[near:] * bits[:, None]], 0)
    table = jnp.sum(level_table.transpose(1, 0, 2)[:, :, None, :] * scaled[None, None], -1)
    table = jnp.pad(table, ((0, 0), (0, 0), (0, HD - table.shape[2])))
    high, low = halves(table)
    return jnp.concatenate([high, low], 1)


def picked_rows(table_index, table_count):
    ids = jnp.arange(2 * table_count, dtype=jnp.int32) % table_count
    column = (table_index[:, None] == ids[None, :]).astype(BF16)
    row = (table_index[None, :] == ids[:, None]).astype(BF16)
    return column, row


def step(queries, keys, values, cotangent, out_weight, level_table, table_index, level_column):
    tok_rows, feature_width = queries.shape
    head_count = feature_width // HD
    ctx_count = lax.axis_size("ctx")
    ctx_bits = ctx_count.bit_length() - 1
    tok_bits = tok_rows.bit_length() - 1
    levels = tok_bits + ctx_bits + 1
    ctx_index = lax.axis_index("ctx")
    head_index = lax.axis_index("head")
    heads = lax.axis_size("head")
    groups = ctx_count // 2
    half = groups // 2
    side = ctx_index & 1
    group = ctx_index >> 1
    wcols = out_weight.shape[1]
    pieces = feature_width // wcols // 2

    running = states_of(keys, values)
    seg_list = []
    for bit in range(ctx_bits):
        last = bit == ctx_bits - 1
        seg = swap(running, "ctx", 1 << bit, upward=last)
        seg_list.append(seg)
        running = (running.astype(F32) + seg.astype(F32)).astype(BF16)

    cot4 = cotangent.reshape(tok_rows, pieces, 2, wcols)
    even, odd = cot4[:, :, 0].reshape(tok_rows, -1), cot4[:, :, 1].reshape(tok_rows, -1)
    kept = jnp.where(side == 0, even, odd)
    sent = jnp.where(side == 0, odd, even)
    came = swap(sent, "ctx", 1)
    cot_pair = jnp.concatenate([kept, came], 0)[None]
    offsets = [0]
    flip = heads // 2
    while flip:
        cot_pair = jnp.concatenate([cot_pair, swap(cot_pair, "head", flip)], 0)
        offsets = offsets + [o ^ flip for o in offsets]
        flip //= 2
    slot_of = {o: i for i, o in enumerate(offsets)}

    def cot_chunk(chunk):
        relative = (chunk // pieces) ^ head_index
        slot = jnp.zeros((), jnp.int32)
        for o, i in slot_of.items():
            slot = jnp.where(relative == o, i, slot)
        part = lax.dynamic_index_in_dim(cot_pair, slot, 0, keepdims=False)
        return lax.dynamic_slice_in_dim(part, (chunk % pieces) * wcols, wcols, 1)

    def clip(index):
        return jnp.clip(index, 0, groups - 1)

    arrivals = [(out_weight, group, True)]
    rising = falling = both = out_weight
    for s in range(1, groups):
        if s > half:
            both = shift(both, groups, (s - 1, groups), (0, groups - s))
        else:
            rising = shift(rising, groups, up=(s - 1, groups))
            falling = shift(falling, groups, down=(0, groups - s))
            both = rising + falling
        below, above = group >= s, group + s < groups
        if s < half:
            arrivals += [(rising, group - s, below), (falling, group + s, above)]
        else:
            arrivals.append((both, jnp.where(below, group - s, group + s), below | above))
    grad_acc = None
    for chunk, index, _ in arrivals:
        product = lax.dot_general(
            cot_chunk(clip(index)), chunk, (((1,), (1,)), ((), ())), preferred_element_type=F32
        )
        grad_acc = product if grad_acc is None else grad_acc + product

    column, row = picked_rows(table_index, level_table.shape[0])
    table = level_tables(level_table, level_column, levels, tok_bits + 1, ctx_bits, ctx_index)
    flipped = table.transpose(0, 2, 1)
    near = near_of(queries, keys, values, column, table)
    attn = far_of(near, queries, column, table, seg_list, levels, head_count, 0)
    attn_came = swap(attn, "ctx", 1)
    attn_pair = jnp.concatenate([attn, attn_came], 0)

    def weight_part(index):
        return lax.dot_general(
            attn_pair, cot_chunk(clip(index)), (((0,), (0,)), ((), ())), preferred_element_type=F32
        )

    up = down = both = None
    for s in range(1, groups):
        if s <= half:
            index = jnp.where(group < half, group + groups - s, group - groups + s)
            rise = weight_part(index)
            if both is not None:
                rise = rise + both.astype(F32)
            rise = fall = rise.astype(BF16)
        else:
            rise = (weight_part(group + groups - s) + up.astype(F32)).astype(BF16)
            fall = (weight_part(group - groups + s) + down.astype(F32)).astype(BF16)
        if 2 * s < groups - 1:
            both = shift(rise, groups, (0, s - 1), (groups - s, groups))
        else:
            up = shift(rise, groups, up=(0, s - 1))
            down = shift(fall, groups, down=(groups - s, groups))
    total = weight_part(group) + up.astype(F32) + down.astype(F32)
    grad_weight = total * (tok_rows * ctx_count) ** (-0.5)

    clear = (1 - (ctx_index >> jnp.arange(ctx_bits) & 1)).astype(F32)
    clear = jnp.broadcast_to(clear[:, None], (ctx_bits, HD))
    theirs = swap(grad_acc[tok_rows:].astype(BF16), "ctx", 1)
    pending, grad = adjoints_of(
        queries, grad_acc[:tok_rows], theirs, row, flipped, tok_bits + 1, ctx_bits, head_count, 0
    )
    found = []
    for bit in range(ctx_bits):
        last = bit == ctx_bits - 1
        partner = swap(pending, "ctx", 1 << bit, downward=last)
        found.append(partner)
        pending = (pending[1:].astype(F32) + partner[1:].astype(F32)).astype(BF16)
    grad_queries, near_dk, near_dv = backward_of(
        queries, keys, values, grad, column, row, table, flipped, seg_list, levels, head_count, 0, ()
    )
    grad_keys, grad_values = finish_of(
        keys, values, near_dk, near_dv, found, clear, head_count, 0, ()
    )

    def chosen_for(order):
        chosen = []
        for o in order:
            for i in range(pieces):
                chunk = (head_index ^ o) * pieces + i
                slot = jnp.zeros((), jnp.int32)
                for k, (_, index, valid) in enumerate(arrivals):
                    slot = jnp.where((chunk == index) & valid, k, slot)
                chosen.append(slot)
        return jnp.stack(chosen)

    sources = [chunk for chunk, _, _ in arrivals]
    away = [o for o in range(heads) if o & 1]
    home = [o ^ 1 for o in away]
    sent = layer_of(chosen_for(away), attn, attn_came, sources)
    came = swap(sent, "head", 1)
    kept = layer_of(chosen_for(home), attn, attn_came, sources, came)
    partials = {o: kept[i * pieces : (i + 1) * pieces] for i, o in enumerate(home)}
    flip = 2
    while flip < heads:
        out_going = sorted(o for o in partials if o & flip)
        sent = jnp.concatenate([partials[o] for o in out_going], 0)
        came = swap(sent, "head", flip)
        partials = {
            o ^ flip: partials[o ^ flip].astype(F32)
            + came[i * pieces : (i + 1) * pieces].astype(F32)
            for i, o in enumerate(out_going)
        }
        partials = {o: x.astype(BF16) for o, x in partials.items()}
        flip *= 2
    layer = partials[0]
    layer_own = layer[:, :tok_rows]
    layer_other = swap(layer[:, tok_rows:], "ctx", 1)
    layer_out = jnp.stack(
        [
            jnp.where(side == 0, layer_own, layer_other),
            jnp.where(side == 0, layer_other, layer_own),
        ],
        1,
    )
    layer_out = layer_out.reshape(2 * pieces, tok_rows, wcols).transpose(1, 0, 2)
    layer_out = layer_out.reshape(tok_rows, feature_width)
    return (layer_out, grad_queries, grad_keys, grad_values, grad_weight)


def solution(mesh):
    placed = (
        P("ctx", "head"),
        P("ctx", "head"),
        P("ctx", "head"),
        P("ctx", "head"),
        P("head", "ctx"),
        P(None, "head", None),
        P("ctx"),
        P(),
    )
    return jax.shard_map(
        step,
        mesh=mesh,
        in_specs=placed,
        out_specs=(
            P("ctx", "head"),
            P("ctx", "head"),
            P("ctx", "head"),
            P("ctx", "head"),
            P("head", "ctx"),
        ),
        check_vma=False,
    )
```

```python
import jax
import jax.numpy as jnp
from jax import lax
from jax.experimental import pallas as pl
from jax.experimental.pallas import tpu as pltpu
from jax.sharding import PartitionSpec as P


HD = 128
F32 = jnp.float32
BF16 = jnp.bfloat16


def route(block, axis, pairs):
    return lax.ppermute(block, axis, pairs)


def swap(block, axis, flip, upward=False, downward=False):
    pairs = [(i, i ^ flip) for i in range(lax.axis_size(axis))]
    if upward:
        pairs = [(i, j) for i, j in pairs if i < j]
    if downward:
        pairs = [(i, j) for i, j in pairs if i > j]
    return route(block, axis, pairs)


def shift(block, groups, up=None, down=None):
    pairs = []
    for step, reach in ((1, up), (-1, down)):
        if reach is None:
            continue
        for group in range(max(reach[0], 0), min(reach[1], groups - 1) + 1):
            if 0 <= group + step < groups:
                pairs += [(2 * group + side, 2 * (group + step) + side) for side in (0, 1)]
    return route(block, "ctx", pairs)


def dot_nn(a, b):
    return lax.dot_general(a, b, (((1,), (0,)), ((), ())), preferred_element_type=F32)


def dot_nt(a, b):
    return lax.dot_general(a, b, (((1,), (1,)), ((), ())), preferred_element_type=F32)


def dot_tn(a, b):
    return lax.dot_general(a, b, (((0,), (0,)), ((), ())), preferred_element_type=F32)


def halves(x):
    high = lax.reduce_precision(x, 8, 7)
    return high.astype(BF16), (x - high).astype(BF16)


def near_blocks(tok_rows):
    blocks = [(at, at, HD, None) for at in range(0, tok_rows, HD)]
    size = HD
    while size < tok_rows:
        level = size.bit_length()
        blocks += [(at + size, at, size, level) for at in range(0, tok_rows, 2 * size)]
        size *= 2
    return blocks


def masks():
    row = lax.broadcasted_iota(jnp.int32, (HD, HD), 0)
    col = lax.broadcasted_iota(jnp.int32, (HD, HD), 1)
    level = jnp.zeros((HD, HD), jnp.int32)
    for bit in range(HD.bit_length() - 1):
        level = level + ((row ^ col) >= 1 << bit).astype(jnp.int32)
    return jnp.where(col <= row, level, HD - 1), level, row <= col


def weight_rows(lam, row, size, level, where):
    part = lam[row : row + size]
    if level is not None:
        return part[:, level : level + 1]
    return jnp.take_along_axis(part, where[0], axis=1, mode="promise_in_bounds")


def weight_cols(lam_t, row, size, level, where):
    part = lam_t[:, row : row + size]
    if level is not None:
        return part[level : level + 1]
    rows = [
        jnp.take_along_axis(part[:8], where[1][i : i + 8], axis=0, mode="promise_in_bounds")
        for i in range(0, HD, 8)
    ]
    return jnp.where(where[2], jnp.concatenate(rows, 0), 0.0)


def add_rows(total, at, part):
    for i in range(0, part.shape[0], HD):
        slot = (at + i) // HD
        piece = part[i : i + HD]
        total[slot] = piece if total[slot] is None else total[slot] + piece


def state_kernel(pack, k_ref, v_ref, o_ref):
    for n in range(pack):
        at = pl.ds(n * HD, HD)
        o_ref[n] = dot_tn(k_ref[:, at], v_ref[:, at]).astype(BF16)


def near_kernel(pack, q_ref, k_ref, v_ref, picked_ref, table_ref, o_ref):
    tok_rows = q_ref.shape[0]
    where = masks()
    for n in range(pack):
        q, k, v = (ref[:, pl.ds(n * HD, HD)] for ref in (q_ref, k_ref, v_ref))
        lam = dot_nn(picked_ref[...], table_ref[n])
        total = [None] * (tok_rows // HD)
        for row, col, size, level in near_blocks(tok_rows):
            weight = weight_rows(lam, row, size, level, where)
            score = dot_nt(q[row : row + size], k[col : col + size])
            add_rows(total, row, dot_nn((weight * score).astype(BF16), v[col : col + size]))
        for i in range(tok_rows // HD):
            o_ref[i * HD : (i + 1) * HD, pl.ds(n * HD, HD)] = total[i]


def far_kernel(pack, far, levels, near_ref, q_ref, picked_ref, table_ref, *refs):
    segs, o_ref = refs[:far], refs[far]
    for n in range(pack):
        lanes = pl.ds(n * HD, HD)
        lam = dot_nn(picked_ref[...], table_ref[n])
        through = dot_nn(q_ref[:, lanes], jnp.concatenate([seg[n] for seg in segs], 1))
        out = near_ref[:, lanes]
        for j in range(far):
            out = out + lam[:, levels + j : levels + j + 1] * through[:, j * HD : (j + 1) * HD]
        o_ref[:, lanes] = out.astype(BF16)


def adjoint_kernel(
    pack, far, near, picked_ref, q_ref, mine_ref, theirs_ref, table_ref, first_ref, rest_ref, g_ref
):
    for n in range(pack):
        lanes = pl.ds(n * HD, HD)
        g = (mine_ref[:, lanes] + theirs_ref[:, lanes].astype(F32)).astype(BF16)
        g_ref[:, lanes] = g
        lam = dot_nn(table_ref[n], picked_ref[...])
        q_t = q_ref[:, lanes].T.astype(F32)
        stacked = jnp.concatenate(
            [(lam[near + j : near + j + 1] * q_t).astype(BF16) for j in range(far)], 0
        )
        found = dot_nn(stacked, g)
        first_ref[0, n] = found[:HD].astype(BF16)
        for j in range(1, far):
            rest_ref[j - 1, n] = found[j * HD : (j + 1) * HD].astype(BF16)


def backward_kernel(
    pack, far, levels, q_ref, k_ref, v_ref, g_ref, column_ref, row_ref, table_ref, flipped_ref, *refs
):
    segs, (dq_ref, dk_ref, dv_ref) = refs[:far], refs[far:]
    tok_rows = q_ref.shape[0]
    where = masks()
    for n in range(pack):
        lanes = pl.ds(n * HD, HD)
        q_all, k_all, v_all, g_all = (ref[:, lanes] for ref in (q_ref, k_ref, v_ref, g_ref))
        lam = dot_nn(column_ref[...], table_ref[n])
        lam_t = dot_nn(flipped_ref[n], row_ref[...])
        dq, dk, dv = ([None] * (tok_rows // HD) for _ in range(3))
        for row, col, size, level in near_blocks(tok_rows):
            q, g = q_all[row : row + size], g_all[row : row + size]
            k, v = k_all[col : col + size], v_all[col : col + size]
            weight = weight_rows(lam, row, size, level, where)
            flipped = weight_cols(lam_t, row, size, level, where)
            add_rows(dq, row, dot_nn((weight * dot_nt(g, v)).astype(BF16), k))
            add_rows(dk, col, dot_nn((flipped * dot_nt(v, g)).astype(BF16), q))
            add_rows(dv, col, dot_nn((flipped * dot_nt(k, q)).astype(BF16), g))
        back = dot_nt(g_all, jnp.concatenate([seg[n] for seg in segs], 0))
        for i in range(tok_rows // HD):
            out = dq[i]
            at = i * HD
            for j in range(far):
                scale = lam[at : at + HD, levels + j : levels + j + 1]
                out = out + scale * back[at : at + HD, j * HD : (j + 1) * HD]
            dq_ref[at : at + HD, lanes] = out.astype(BF16)
            dk_ref[at : at + HD, lanes] = dk[i]
            dv_ref[at : at + HD, lanes] = dv[i]


def finish_kernel(pack, far, clear_ref, k_ref, v_ref, dk_ref, dv_ref, *refs):
    found, (dk_out, dv_out) = refs[:far], refs[far:]
    for n in range(pack):
        lanes = pl.ds(n * HD, HD)
        adjoint = clear_ref[0:1] * found[0][0, n].astype(F32)
        for j in range(1, far):
            adjoint = adjoint + clear_ref[j : j + 1] * found[j][0, n].astype(F32)
        adjoint = adjoint.astype(BF16)
        dk_out[:, lanes] = (dk_ref[:, lanes] + dot_nt(v_ref[:, lanes], adjoint)).astype(BF16)
        dv_out[:, lanes] = (dv_ref[:, lanes] + dot_nn(k_ref[:, lanes], adjoint)).astype(BF16)


def shape(dims, kind):
    return jax.ShapeDtypeStruct(dims, kind)


def per_head(kernel, most, flops, heads, first, ins, outs, consts=(), into=()):
    pack = min(most, heads)

    def spec(x):
        if len(x.shape) == 2:
            at = first // pack if x.shape[1] > heads * HD else 0
            return pl.BlockSpec((ins[0].shape[0], pack * HD), lambda h: (0, h + at))
        at = first // pack if x.shape[-3] > heads else 0
        lead = (0,) * (len(x.shape) - 3)
        return pl.BlockSpec(x.shape[:-3] + (pack,) + x.shape[-2:], lambda h: lead + (h + at, 0, 0))

    def run(*refs):
        kernel(pack, *refs[len(into) :])

    size = flops // HD + sum(x.size * x.dtype.itemsize for x in outs)
    whole = [pl.BlockSpec(x.shape, lambda h: (0, 0)) for x in consts]
    kept = [pl.BlockSpec(memory_space=pl.ANY)] * len(into)
    single = len(outs) == 1
    return pl.pallas_call(
        run,
        grid=(heads // pack,),
        in_specs=kept + whole + [spec(x) for x in ins],
        out_specs=spec(outs[0]) if single else [spec(x) for x in outs],
        out_shape=outs[0] if single else list(outs),
        input_output_aliases={i: i for i in range(len(into))},
        cost_estimate=pl.CostEstimate(flops=flops, bytes_accessed=size, transcendentals=0),
    )(*into, *consts, *ins)


def states_of(keys, values):
    rows, width = keys.shape
    heads = width // HD
    return per_head(
        state_kernel, 4, 2 * rows * width * HD, heads, 0,
        (keys, values), (shape((heads, HD, HD), BF16),),
    )


def near_of(queries, keys, values, column, table):
    rows, width = queries.shape

    def kernel(pack, picked, q, k, v, table, out):
        near_kernel(pack, q, k, v, picked, table, out)

    return per_head(
        kernel, 2, 6 * rows * rows * width, width // HD, 0,
        (queries, keys, values, table), (shape((rows, width), F32),), (column,),
    )


def far_of(near, queries, column, table, segs, levels, heads, first):
    rows = queries.shape[0]

    def kernel(pack, picked, *refs):
        far_kernel(pack, len(segs), levels, *refs[:2], picked, *refs[2:])

    return per_head(
        kernel, 2, 2 * len(segs) * rows * heads * HD * HD, heads, first,
        (near, queries, table, *segs), (shape((rows, heads * HD), BF16),), (column,),
    )


def adjoints_of(queries, mine, theirs, row, flipped, near, far, heads, first):
    rows = queries.shape[0]

    def kernel(pack, *refs):
        adjoint_kernel(pack, far, near, *refs)

    return per_head(
        kernel, 4, 2 * far * rows * heads * HD * HD, heads, first,
        (queries, mine, theirs, flipped),
        (
            shape((1, heads, HD, HD), BF16),
            shape((far - 1, heads, HD, HD), BF16),
            shape((rows, heads * HD), BF16),
        ),
        (row,),
    )


def backward_of(queries, keys, values, grad, column, row, table, flipped, segs, levels, heads, first, into):
    rows, width = queries.shape

    def kernel(pack, column, row, *refs):
        backward_kernel(pack, len(segs), levels, *refs[:4], column, row, *refs[4:])

    part = shape((rows, heads * HD), F32)
    return per_head(
        kernel, 2, 12 * rows * rows * heads * HD, heads, first,
        (queries, keys, values, grad, table, flipped, *segs),
        (shape((rows, width), BF16), part, part), (column, row), into,
    )


def finish_of(keys, values, dk, dv, found, clear, heads, first, into):
    rows, width = keys.shape

    def kernel(pack, *refs):
        finish_kernel(pack, len(found), *refs)

    return per_head(
        kernel, 4, 4 * rows * heads * HD * HD, heads, first,
        (keys, values, dk, dv, *found), (shape((rows, width), BF16),) * 2, (clear,), into,
    )


def layer_kernel(sources, adds, tile, chosen_ref, mine_ref, theirs_ref, *refs):
    weights, came, outs = refs[:sources], refs[sources : sources + adds], refs[sources + adds : -2]
    held, sems = refs[-2:]
    step, count = pl.program_id(0), pl.num_programs(0)

    def fetch(entry, slot):
        for i in range(sources):

            @pl.when(chosen_ref[entry] == i)
            def _(i=i):
                pltpu.make_async_copy(weights[i], held.at[slot], sems.at[slot]).start()

    @pl.when(step == 0)
    def _():
        fetch(0, 0)

    @pl.when(step + 1 < count)
    def _():
        fetch(step + 1, (step + 1) % 2)

    now = step % 2
    pltpu.make_async_copy(weights[0], held.at[now], sems.at[now]).wait()
    rows = mine_ref.shape[0]
    for entry, o_ref in enumerate(outs):

        @pl.when(step == entry)
        def _(o_ref=o_ref, entry=entry):
            for k, ref in enumerate((mine_ref, theirs_ref)):
                for at in range(0, rows, tile):
                    total = dot_nn(ref[at : at + tile], held[now])
                    into = slice(k * rows + at, k * rows + at + tile)
                    if adds:
                        total = total + came[entry][into].astype(F32)
                    o_ref[into] = total.astype(BF16)


def layer_of(chosen, mine, theirs, weights, came=(), tile=256):
    rows, width = mine.shape
    count, cols = chosen.shape[0], weights[0].shape[1]

    def whole(dims):
        return pl.BlockSpec(dims, lambda j, c: (0, 0), pipeline_mode=pl.Buffered(1))

    def kernel(*refs):
        layer_kernel(len(weights), len(came), min(tile, rows), *refs)

    return pl.pallas_call(
        kernel,
        grid_spec=pltpu.PrefetchScalarGridSpec(
            num_scalar_prefetch=1,
            grid=(count,),
            in_specs=[whole(mine.shape)] * 2
            + [pl.BlockSpec(memory_space=pl.ANY)] * len(weights)
            + [whole((2 * rows, cols))] * len(came),
            out_specs=[whole((2 * rows, cols))] * count,
            scratch_shapes=[
                pltpu.VMEM((2,) + weights[0].shape, BF16),
                pltpu.SemaphoreType.DMA((2,)),
            ],
        ),
        out_shape=[shape((2 * rows, cols), BF16)] * count,
        name="layer",
        cost_estimate=pl.CostEstimate(
            flops=4 * count * rows * width * cols, bytes_accessed=4 * count * rows * cols, transcendentals=0
        ),
    )(chosen, mine, theirs, *weights, *came)


def level_scales(levels):
    level_ids = jnp.arange(levels, dtype=jnp.float32)
    return jnp.where(level_ids < 0.5, 1.0, jnp.exp2(-(level_ids - 1.0) * 0.5))


def level_tables(level_table, level_column, levels, near, ctx_bits, ctx_index):
    columns = (
        level_column[:levels, None] == jnp.arange(level_table.shape[2], dtype=jnp.int32)[None, :]
    ).astype(F32)
    scaled = columns * (level_scales(levels) * HD ** (-0.5))[:, None]
    bits = (ctx_index >> jnp.arange(ctx_bits, dtype=jnp.int32) & 1).astype(F32)
    scaled = jnp.concatenate([scaled, scaled[near:] * bits[:, None]], 0)
    table = jnp.sum(level_table.transpose(1, 0, 2)[:, :, None, :] * scaled[None, None], -1)
    table = jnp.pad(table, ((0, 0), (0, 0), (0, HD - table.shape[2])))
    high, low = halves(table)
    return jnp.concatenate([high, low], 1)


def picked_rows(table_index, table_count):
    ids = jnp.arange(2 * table_count, dtype=jnp.int32) % table_count
    column = (table_index[:, None] == ids[None, :]).astype(BF16)
    row = (table_index[None, :] == ids[:, None]).astype(BF16)
    return column, row


def step(queries, keys, values, cotangent, out_weight, level_table, table_index, level_column):
    tok_rows, feature_width = queries.shape
    head_count = feature_width // HD
    ctx_count = lax.axis_size("ctx")
    ctx_bits = ctx_count.bit_length() - 1
    tok_bits = tok_rows.bit_length() - 1
    levels = tok_bits + ctx_bits + 1
    ctx_index = lax.axis_index("ctx")
    head_index = lax.axis_index("head")
    heads = lax.axis_size("head")
    groups = ctx_count // 2
    half = groups // 2
    side = ctx_index & 1
    group = ctx_index >> 1
    wcols = out_weight.shape[1]
    pieces = feature_width // wcols // 2

    running = states_of(keys, values)
    seg_list = []
    for bit in range(ctx_bits - 1):
        seg = swap(running, "ctx", 1 << bit, upward=0 < bit == ctx_bits - 2)
        seg_list.append(seg)
        running = (running.astype(F32) + seg.astype(F32)).astype(BF16)
    seg = None
    for k in range(half):
        running = shift(running, groups, up=(half - 1 + k, half - 1 + k))
        seg = running if seg is None else seg + running
    seg_list.append(seg)

    def columns_of(which):
        found = [
            lax.dynamic_slice_in_dim(cotangent, (2 * m + which) * wcols, wcols, 1)
            for m in range(pieces)
        ]
        return found[0] if pieces == 1 else jnp.concatenate(found, 1)

    kept, sent = columns_of(side), columns_of(1 - side)
    came = swap(sent, "ctx", 1)
    flip = heads // 2
    far_kept = swap(kept, "head", flip)
    far_came = swap(came, "head", flip)
    cot_pair = jnp.stack([kept, came, far_kept, far_came], 0).reshape(2, 2, tok_rows, -1)
    offsets = [0, flip]
    flip //= 2
    while flip:
        cot_pair = jnp.concatenate([cot_pair, swap(cot_pair, "head", flip)], 0)
        offsets = offsets + [o ^ flip for o in offsets]
        flip //= 2
    cot_pair = cot_pair.reshape(heads, 2 * tok_rows, -1)
    slot_of = {o: i for i, o in enumerate(offsets)}

    def cot_chunk(chunk):
        relative = (chunk // pieces) ^ head_index
        slot = jnp.zeros((), jnp.int32)
        for o, i in slot_of.items():
            slot = jnp.where(relative == o, i, slot)
        part = lax.dynamic_index_in_dim(cot_pair, slot, 0, keepdims=False)
        return lax.dynamic_slice_in_dim(part, (chunk % pieces) * wcols, wcols, 1)

    def clip(index):
        return jnp.clip(index, 0, groups - 1)

    arrivals = [(out_weight, group, True)]
    rising = falling = both = out_weight
    for s in range(1, groups):
        if s > half:
            both = shift(both, groups, (s - 1, groups), (0, groups - s))
        else:
            rising = shift(rising, groups, up=(s - 1, groups))
            falling = shift(falling, groups, down=(0, groups - s))
            both = rising + falling
        below, above = group >= s, group + s < groups
        if s < half:
            arrivals += [(rising, group - s, below), (falling, group + s, above)]
        else:
            arrivals.append((both, jnp.where(below, group - s, group + s), below | above))
    grad_both = 0.0
    for chunk, index, _ in arrivals[:-1]:
        grad_both += dot_nt(cot_chunk(clip(index)), chunk)
    grad_both = lax.optimization_barrier(grad_both)
    chunk, index, _ = arrivals[-1]
    part = cot_chunk(clip(index))[tok_rows:]
    grad_theirs = (grad_both[tok_rows:] + dot_nt(part, chunk)).astype(BF16)
    theirs = swap(grad_theirs, "ctx", 1)
    part = cot_chunk(clip(index))[:tok_rows]
    grad_mine = grad_both[:tok_rows] + dot_nt(part, chunk)

    column, row = picked_rows(table_index, level_table.shape[0])
    table = level_tables(level_table, level_column, levels, tok_bits + 1, ctx_bits, ctx_index)
    flipped = table.transpose(0, 2, 1)
    near = near_of(queries, keys, values, column, table)
    attn = far_of(near, queries, column, table, seg_list, levels, head_count, 0)
    attn_came = swap(attn, "ctx", 1)
    attn_pair = jnp.concatenate([attn, attn_came], 0)

    def weight_part(index):
        return lax.dot_general(
            attn_pair, cot_chunk(clip(index)), (((0,), (0,)), ((), ())), preferred_element_type=F32
        )

    products = []
    for s in range(1, groups + 1):
        going_up, going_down = group + groups - s, group - groups + s
        if s == groups:
            wanted = [group]
        elif s <= half:
            wanted = [jnp.where(group < half, going_up, going_down)]
        else:
            wanted = [going_up, going_down]
        products.append([weight_part(index) for index in wanted])
    products[1:] = [[lax.optimization_barrier(x) for x in found] for found in products[1:]]
    up = down = both = None
    for s in range(1, groups):
        found = products[s - 1]
        if s <= half:
            rise = found[0] if both is None else found[0] + both.astype(F32)
            rise = fall = rise.astype(BF16)
        else:
            rise = (found[0] + up.astype(F32)).astype(BF16)
            fall = (found[1] + down.astype(F32)).astype(BF16)
        if 2 * s < groups - 1:
            both = shift(rise, groups, (0, s - 1), (groups - s, groups))
        else:
            up = shift(rise, groups, up=(0, s - 1))
            down = shift(fall, groups, down=(groups - s, groups))
    total = products[-1][0] + up.astype(F32) + down.astype(F32)
    grad_weight = total * (tok_rows * ctx_count) ** (-0.5)

    clear = (1 - (ctx_index >> jnp.arange(ctx_bits) & 1)).astype(F32)
    clear = jnp.broadcast_to(clear[:, None], (ctx_bits, HD))
    first, pending, grad = adjoints_of(
        queries, grad_mine, theirs, row, flipped, tok_bits + 1, ctx_bits, head_count, 0
    )
    partner = swap(pending, "ctx", 1)
    found = [swap(first, "ctx", 1, downward=True)]
    pending = (pending.astype(F32) + partner.astype(F32)).astype(BF16)
    for bit in range(1, ctx_bits - 1):
        partner = swap(pending, "ctx", 1 << bit, downward=bit == ctx_bits - 2)
        found.append(partner)
        pending = (pending[1:].astype(F32) + partner[1:].astype(F32)).astype(BF16)
    partner = None
    for k in range(half):
        pending = shift(pending, groups, down=(half - k, half - k))
        partner = pending if partner is None else partner + pending
    found.append(partner)
    parts = 1
    part_heads = head_count // parts
    into_q, nears = (), []
    for p in range(parts):
        grad_queries, *pair = backward_of(
            queries, keys, values, grad, column, row, table, flipped, seg_list, levels,
            part_heads, p * part_heads, into_q,
        )
        into_q = (grad_queries,)
        nears.append(pair)
    into_kv = ()
    for p in range(parts):
        into_kv = tuple(
            finish_of(keys, values, *nears[p], found, clear, part_heads, p * part_heads, into_kv)
        )
    grad_keys, grad_values = into_kv

    def chosen_for(order):
        chosen = []
        for o in order:
            for i in range(pieces):
                chunk = (head_index ^ o) * pieces + i
                slot = jnp.zeros((), jnp.int32)
                for k, (_, index, valid) in enumerate(arrivals):
                    slot = jnp.where((chunk == index) & valid, k, slot)
                chosen.append(slot)
        return jnp.stack(chosen)

    sources = [chunk for chunk, _, _ in arrivals]
    away = [o for o in range(heads) if o & 1]
    home = [o ^ 1 for o in away]
    sent = layer_of(chosen_for(away), attn, attn_came, sources)
    came = []
    for x in sent:
        came.append(swap(x, "head", 1))
    kept = layer_of(chosen_for(home), attn, attn_came, sources, came)
    partials = {o: kept[i * pieces : (i + 1) * pieces] for i, o in enumerate(home)}
    flip = 2
    while flip < heads:
        out_going = sorted(o for o in partials if o & flip)
        summed = {}
        for o in out_going:
            found = []
            for i in range(pieces):
                came = swap(partials[o][i], "head", flip)
                total = partials[o ^ flip][i].astype(F32) + came.astype(F32)
                found.append(total.astype(BF16))
            summed[o ^ flip] = found
        partials = summed
        flip *= 2
    sent = jnp.concatenate([x[tok_rows:] for x in partials[0]], 1)
    other = swap(sent, "ctx", 1)
    columns = []
    for i, x in enumerate(partials[0]):
        own, theirs = x[:tok_rows], other[:, i * wcols : (i + 1) * wcols]
        columns += [jnp.where(side == 0, own, theirs), jnp.where(side == 0, theirs, own)]
    layer_out = jnp.concatenate(columns, 1)
    return (layer_out, grad_queries, grad_keys, grad_values, grad_weight)


def solution(mesh):
    placed = (
        P("ctx", "head"),
        P("ctx", "head"),
        P("ctx", "head"),
        P("ctx", "head"),
        P("head", "ctx"),
        P(None, "head", None),
        P("ctx"),
        P(),
    )
    return jax.shard_map(
        step,
        mesh=mesh,
        in_specs=placed,
        out_specs=(
            P("ctx", "head"),
            P("ctx", "head"),
            P("ctx", "head"),
            P("ctx", "head"),
            P("head", "ctx"),
        ),
        check_vma=False,
    )
```

```python
import jax
import jax.numpy as jnp
from jax import lax
from jax.experimental import pallas as pl
from jax.experimental.pallas import tpu as pltpu
from jax.sharding import PartitionSpec as P


HD = 128
F32 = jnp.float32
BF16 = jnp.bfloat16


def route(block, axis, pairs):
    return lax.ppermute(block, axis, pairs)


def swap(block, axis, flip, upward=False, downward=False):
    pairs = [(i, i ^ flip) for i in range(lax.axis_size(axis))]
    if upward:
        pairs = [(i, j) for i, j in pairs if i < j]
    if downward:
        pairs = [(i, j) for i, j in pairs if i > j]
    return route(block, axis, pairs)


def shift(block, groups, up=None, down=None):
    pairs = []
    for step, reach in ((1, up), (-1, down)):
        if reach is None:
            continue
        for group in range(max(reach[0], 0), min(reach[1], groups - 1) + 1):
            if 0 <= group + step < groups:
                pairs += [(2 * group + side, 2 * (group + step) + side) for side in (0, 1)]
    return route(block, "ctx", pairs)


def dot_nn(a, b):
    return lax.dot_general(a, b, (((1,), (0,)), ((), ())), preferred_element_type=F32)


def dot_nt(a, b):
    return lax.dot_general(a, b, (((1,), (1,)), ((), ())), preferred_element_type=F32)


def dot_tn(a, b):
    return lax.dot_general(a, b, (((0,), (0,)), ((), ())), preferred_element_type=F32)


def post(block, source, target):
    return route(block, "ctx", [(2 * source + side, 2 * target + side) for side in (0, 1)])


def sum_of(terms):
    total = terms[0].astype(F32)
    for term in terms[1:]:
        total = total + term.astype(F32)
    return total.astype(BF16)


def halves(x):
    high = lax.reduce_precision(x, 8, 7)
    return high.astype(BF16), (x - high).astype(BF16)


def near_blocks(tok_rows):
    base = min(2 * HD, tok_rows)
    blocks = [(at, at, base, None) for at in range(0, tok_rows, base)]
    size = base
    while size < tok_rows:
        level = size.bit_length()
        blocks += [(at + size, at, size, level) for at in range(0, tok_rows, 2 * size)]
        size *= 2
    return blocks


def masks():
    row = lax.broadcasted_iota(jnp.int32, (HD, HD), 0)
    col = lax.broadcasted_iota(jnp.int32, (HD, HD), 1)
    level = jnp.zeros((HD, HD), jnp.int32)
    for bit in range(HD.bit_length() - 1):
        level = level + ((row ^ col) >= 1 << bit).astype(jnp.int32)
    return jnp.where(col <= row, level, HD - 1), level, row <= col


def tiled(tiles, flip):
    first, cross, second = tiles
    blank = jnp.zeros((HD, HD), F32)
    if flip:
        upper, lower = (first, cross), (blank, second)
    else:
        upper, lower = (first, blank), (cross, second)
    return jnp.concatenate([jnp.concatenate(upper, 1), jnp.concatenate(lower, 1)], 0)


def weight_rows(lam, row, size, level, where):
    if level is not None:
        return lam[row : row + size, level : level + 1]

    def tile(at):
        return jnp.take_along_axis(lam[at : at + HD], where[0], axis=1, mode="promise_in_bounds")

    if size == HD:
        return tile(row)
    level = HD.bit_length()
    cross = jnp.broadcast_to(lam[row + HD : row + size, level : level + 1], (HD, HD))
    return tiled((tile(row), cross, tile(row + HD)), False)


def weight_cols(lam_t, row, size, level, where):
    if level is not None:
        return lam_t[level : level + 1, row : row + size]

    def tile(at):
        found = [
            jnp.take_along_axis(
                lam_t[:8, at : at + HD], where[1][i : i + 8], axis=0, mode="promise_in_bounds"
            )
            for i in range(0, HD, 8)
        ]
        return jnp.where(where[2], jnp.concatenate(found, 0), 0.0)

    if size == HD:
        return tile(row)
    level = HD.bit_length()
    cross = jnp.broadcast_to(lam_t[level : level + 1, row + HD : row + size], (HD, HD))
    return tiled((tile(row), cross, tile(row + HD)), True)


def add_rows(total, at, part):
    for i in range(0, part.shape[0], HD):
        slot = (at + i) // HD
        piece = part[i : i + HD]
        total[slot] = piece if total[slot] is None else total[slot] + piece


def state_kernel(pack, k_ref, v_ref, o_ref):
    for n in range(pack):
        at = pl.ds(n * HD, HD)
        o_ref[n] = dot_tn(k_ref[:, at], v_ref[:, at]).astype(BF16)


def near_kernel(pack, q_ref, k_ref, v_ref, picked_ref, table_ref, o_ref):
    tok_rows = q_ref.shape[0]
    where = masks()
    for n in range(pack):
        q, k, v = (ref[:, pl.ds(n * HD, HD)] for ref in (q_ref, k_ref, v_ref))
        lam = dot_nn(picked_ref[...], table_ref[n])
        total = [None] * (tok_rows // HD)
        for row, col, size, level in near_blocks(tok_rows):
            weight = weight_rows(lam, row, size, level, where)
            score = dot_nt(q[row : row + size], k[col : col + size])
            add_rows(total, row, dot_nn((weight * score).astype(BF16), v[col : col + size]))
        for i in range(tok_rows // HD):
            o_ref[i * HD : (i + 1) * HD, pl.ds(n * HD, HD)] = total[i]


def far_kernel(pack, far, levels, near_ref, q_ref, picked_ref, table_ref, *refs):
    segs, o_ref = refs[:far], refs[far]
    for n in range(pack):
        lanes = pl.ds(n * HD, HD)
        lam = dot_nn(picked_ref[...], table_ref[n])
        through = dot_nn(q_ref[:, lanes], jnp.concatenate([seg[n] for seg in segs], 1))
        out = near_ref[:, lanes]
        for j in range(far):
            out = out + lam[:, levels + j : levels + j + 1] * through[:, j * HD : (j + 1) * HD]
        o_ref[:, lanes] = out.astype(BF16)


def adjoint_kernel(
    pack, far, near, picked_ref, q_ref, mine_ref, theirs_ref, table_ref, first_ref, rest_ref, g_ref
):
    for n in range(pack):
        lanes = pl.ds(n * HD, HD)
        g = (mine_ref[:, lanes] + theirs_ref[:, lanes].astype(F32)).astype(BF16)
        g_ref[:, lanes] = g
        lam = dot_nn(table_ref[n], picked_ref[...])
        q_t = q_ref[:, lanes].T.astype(F32)
        stacked = jnp.concatenate(
            [(lam[near + j : near + j + 1] * q_t).astype(BF16) for j in range(far)], 0
        )
        found = dot_nn(stacked, g)
        first_ref[0, n] = found[:HD].astype(BF16)
        for j in range(1, far):
            rest_ref[j - 1, n] = found[j * HD : (j + 1) * HD].astype(BF16)


def backward_kernel(
    pack, far, levels, q_ref, k_ref, v_ref, g_ref, column_ref, row_ref, table_ref, flipped_ref, *refs
):
    segs, (dq_ref, dk_ref, dv_ref) = refs[:far], refs[far:]
    tok_rows = q_ref.shape[0]
    where = masks()
    for n in range(pack):
        lanes = pl.ds(n * HD, HD)
        q_all, k_all, v_all, g_all = (ref[:, lanes] for ref in (q_ref, k_ref, v_ref, g_ref))
        lam = dot_nn(column_ref[...], table_ref[n])
        lam_t = dot_nn(flipped_ref[n], row_ref[...])
        dq, dk, dv = ([None] * (tok_rows // HD) for _ in range(3))
        for row, col, size, level in near_blocks(tok_rows):
            q, g = q_all[row : row + size], g_all[row : row + size]
            k, v = k_all[col : col + size], v_all[col : col + size]
            weight = weight_rows(lam, row, size, level, where)
            flipped = weight_cols(lam_t, row, size, level, where)
            add_rows(dq, row, dot_nn((weight * dot_nt(g, v)).astype(BF16), k))
            add_rows(dk, col, dot_nn((flipped * dot_nt(v, g)).astype(BF16), q))
            add_rows(dv, col, dot_nn((flipped * dot_nt(k, q)).astype(BF16), g))
        back = dot_nt(g_all, jnp.concatenate([seg[n] for seg in segs], 0))
        for i in range(tok_rows // HD):
            out = dq[i]
            at = i * HD
            for j in range(far):
                scale = lam[at : at + HD, levels + j : levels + j + 1]
                out = out + scale * back[at : at + HD, j * HD : (j + 1) * HD]
            dq_ref[at : at + HD, lanes] = out.astype(BF16)
            dk_ref[at : at + HD, lanes] = dk[i].astype(BF16)
            dv_ref[at : at + HD, lanes] = dv[i].astype(BF16)


def finish_kernel(pack, far, clear_ref, k_ref, v_ref, dk_ref, dv_ref, *refs):
    found, (dk_out, dv_out) = refs[:far], refs[far:]
    for n in range(pack):
        lanes = pl.ds(n * HD, HD)
        adjoint = clear_ref[0:1] * found[0][0, n].astype(F32)
        for j in range(1, far):
            adjoint = adjoint + clear_ref[j : j + 1] * found[j][0, n].astype(F32)
        adjoint = adjoint.astype(BF16)
        dk_out[:, lanes] = (dk_ref[:, lanes].astype(F32) + dot_nt(v_ref[:, lanes], adjoint)).astype(BF16)
        dv_out[:, lanes] = (dv_ref[:, lanes].astype(F32) + dot_nn(k_ref[:, lanes], adjoint)).astype(BF16)


def shape(dims, kind):
    return jax.ShapeDtypeStruct(dims, kind)


def per_head(kernel, most, flops, heads, first, ins, outs, consts=(), into=()):
    pack = min(most, heads)

    def spec(x):
        if len(x.shape) == 2:
            at = first // pack if x.shape[1] > heads * HD else 0
            return pl.BlockSpec((ins[0].shape[0], pack * HD), lambda h: (0, h + at))
        at = first // pack if x.shape[-3] > heads else 0
        lead = (0,) * (len(x.shape) - 3)
        return pl.BlockSpec(x.shape[:-3] + (pack,) + x.shape[-2:], lambda h: lead + (h + at, 0, 0))

    def run(*refs):
        kernel(pack, *refs[len(into) :])

    size = flops // HD + sum(x.size * x.dtype.itemsize for x in outs)
    whole = [pl.BlockSpec(x.shape, lambda h: (0, 0)) for x in consts]
    kept = [pl.BlockSpec(memory_space=pl.ANY)] * len(into)
    single = len(outs) == 1
    return pl.pallas_call(
        run,
        grid=(heads // pack,),
        in_specs=kept + whole + [spec(x) for x in ins],
        out_specs=spec(outs[0]) if single else [spec(x) for x in outs],
        out_shape=outs[0] if single else list(outs),
        input_output_aliases={i: i for i in range(len(into))},
        cost_estimate=pl.CostEstimate(flops=flops, bytes_accessed=size, transcendentals=0),
    )(*into, *consts, *ins)


def states_of(keys, values):
    rows, width = keys.shape
    heads = width // HD
    return per_head(
        state_kernel, 4, 2 * rows * width * HD, heads, 0,
        (keys, values), (shape((heads, HD, HD), BF16),),
    )


def near_of(queries, keys, values, column, table):
    rows, width = queries.shape

    def kernel(pack, picked, q, k, v, table, out):
        near_kernel(pack, q, k, v, picked, table, out)

    return per_head(
        kernel, 2, 6 * rows * rows * width, width // HD, 0,
        (queries, keys, values, table), (shape((rows, width), F32),), (column,),
    )


def far_of(near, queries, column, table, segs, levels, heads, first):
    rows = queries.shape[0]

    def kernel(pack, picked, *refs):
        far_kernel(pack, len(segs), levels, *refs[:2], picked, *refs[2:])

    return per_head(
        kernel, 2, 2 * len(segs) * rows * heads * HD * HD, heads, first,
        (near, queries, table, *segs), (shape((rows, heads * HD), BF16),), (column,),
    )


def adjoints_of(queries, mine, theirs, row, flipped, near, far, heads, first):
    rows = queries.shape[0]

    def kernel(pack, *refs):
        adjoint_kernel(pack, far, near, *refs)

    return per_head(
        kernel, 4, 2 * far * rows * heads * HD * HD, heads, first,
        (queries, mine, theirs, flipped),
        (
            shape((1, heads, HD, HD), BF16),
            shape((far - 1, heads, HD, HD), BF16),
            shape((rows, heads * HD), BF16),
        ),
        (row,),
    )


def backward_of(queries, keys, values, grad, column, row, table, flipped, segs, levels, heads, first, into):
    rows, width = queries.shape

    def kernel(pack, column, row, *refs):
        backward_kernel(pack, len(segs), levels, *refs[:4], column, row, *refs[4:])

    part = shape((rows, width), BF16)
    return per_head(
        kernel, 2, 12 * rows * rows * heads * HD, heads, first,
        (queries, keys, values, grad, table, flipped, *segs),
        (shape((rows, width), BF16), part, part), (column, row), into,
    )


def finish_of(keys, values, dk, dv, found, clear, heads, first, into):
    rows, width = keys.shape

    def kernel(pack, *refs):
        finish_kernel(pack, len(found), *refs)

    return per_head(
        kernel, 4, 4 * rows * heads * HD * HD, heads, first,
        (keys, values, dk, dv, *found), (shape((rows, width), BF16),) * 2, (clear,), into,
    )


def layer_kernel(sources, adds, tile, chosen_ref, mine_ref, *refs):
    both_ref, weights, came = refs[0], refs[1 : 1 + sources], refs[1 + sources : 1 + sources + adds]
    outs, (other, held, sems, other_sem) = refs[1 + sources + adds : -4], refs[-4:]
    entry, part = pl.program_id(0), pl.program_id(1)
    count = pl.num_programs(0)

    def fetch(which, slot):
        for i in range(sources):

            @pl.when(chosen_ref[which] == i)
            def _(i=i):
                pltpu.make_async_copy(weights[i], held.at[slot], sems.at[slot]).start()

    now = entry % 2
    rows = mine_ref.shape[0]
    rest = pltpu.make_async_copy(both_ref.at[pl.ds(rows, rows)], other, other_sem)

    @pl.when((entry == 0) & (part == 0))
    def _():
        fetch(0, 0)
        rest.start()

    @pl.when((part == 0) & (entry + 1 < count))
    def _():
        fetch(entry + 1, (entry + 1) % 2)

    @pl.when(part == 0)
    def _():
        pltpu.make_async_copy(weights[0], held.at[now], sems.at[now]).wait()

    @pl.when((entry == 0) & (part == 1))
    def _():
        rest.wait()

    for i, o_ref in enumerate(outs):
        for k, ref in enumerate((mine_ref, other)):

            @pl.when((entry == i) & (part == k))
            def _(o_ref=o_ref, i=i, ref=ref):
                for at in range(0, rows, tile):
                    total = dot_nn(ref[at : at + tile], held[now])
                    if adds:
                        total = total + came[i][at : at + tile].astype(F32)
                    o_ref[at : at + tile] = total.astype(BF16)


def layer_of(chosen, pair, weights, came=(), tile=256):
    rows, width = pair.shape[0] // 2, pair.shape[1]
    count, cols = chosen.shape[0], weights[0].shape[1]

    def turn(i):
        return pl.BlockSpec((rows, cols), lambda j, k, c: (jnp.clip(2 * (j - i) + k, 0, 1), 0))

    def kernel(*refs):
        layer_kernel(len(weights), len(came), min(tile, rows), *refs)

    return pl.pallas_call(
        kernel,
        grid_spec=pltpu.PrefetchScalarGridSpec(
            num_scalar_prefetch=1,
            grid=(count, 2),
            in_specs=[
                pl.BlockSpec((rows, width), lambda j, k, c: (0, 0), pipeline_mode=pl.Buffered(1))
            ]
            + [pl.BlockSpec(memory_space=pl.ANY)] * (1 + len(weights))
            + [turn(i) for i in range(len(came))],
            out_specs=[turn(i) for i in range(count)],
            scratch_shapes=[
                pltpu.VMEM((rows, width), BF16),
                pltpu.VMEM((2,) + weights[0].shape, BF16),
                pltpu.SemaphoreType.DMA((2,)),
                pltpu.SemaphoreType.DMA,
            ],
        ),
        out_shape=[shape((2 * rows, cols), BF16)] * count,
        name="layer",
        cost_estimate=pl.CostEstimate(
            flops=4 * count * rows * width * cols, bytes_accessed=4 * count * rows * cols, transcendentals=0
        ),
    )(chosen, pair, pair, *weights, *came)


def level_scales(levels):
    level_ids = jnp.arange(levels, dtype=jnp.float32)
    return jnp.where(level_ids < 0.5, 1.0, jnp.exp2(-(level_ids - 1.0) * 0.5))


def level_tables(level_table, level_column, levels, near, ctx_bits, ctx_index):
    columns = (
        level_column[:levels, None] == jnp.arange(level_table.shape[2], dtype=jnp.int32)[None, :]
    ).astype(F32)
    scaled = columns * (level_scales(levels) * HD ** (-0.5))[:, None]
    bits = (ctx_index >> jnp.arange(ctx_bits, dtype=jnp.int32) & 1).astype(F32)
    scaled = jnp.concatenate([scaled, scaled[near:] * bits[:, None]], 0)
    table = jnp.sum(level_table.transpose(1, 0, 2)[:, :, None, :] * scaled[None, None], -1)
    table = jnp.pad(table, ((0, 0), (0, 0), (0, HD - table.shape[2])))
    high, low = halves(table)
    return jnp.concatenate([high, low], 1)


def picked_rows(table_index, table_count):
    ids = jnp.arange(2 * table_count, dtype=jnp.int32) % table_count
    column = (table_index[:, None] == ids[None, :]).astype(BF16)
    row = (table_index[None, :] == ids[:, None]).astype(BF16)
    return column, row


def step(queries, keys, values, cotangent, out_weight, level_table, table_index, level_column):
    tok_rows, feature_width = queries.shape
    head_count = feature_width // HD
    ctx_count = lax.axis_size("ctx")
    ctx_bits = ctx_count.bit_length() - 1
    tok_bits = tok_rows.bit_length() - 1
    levels = tok_bits + ctx_bits + 1
    ctx_index = lax.axis_index("ctx")
    head_index = lax.axis_index("head")
    heads = lax.axis_size("head")
    groups = ctx_count // 2
    half = groups // 2
    side = ctx_index & 1
    group = ctx_index >> 1
    wcols = out_weight.shape[1]
    pieces = feature_width // wcols // 2

    running = states_of(keys, values)
    seg_list = []
    for bit in range(ctx_bits - 1):
        seg = swap(running, "ctx", 1 << bit, upward=0 < bit == ctx_bits - 2)
        seg_list.append(seg)
        running = (running.astype(F32) + seg.astype(F32)).astype(BF16)
    seg = None
    for k in range(half):
        sent = post(running, half - 1, groups - 1 - k)
        seg = sent if seg is None else seg + sent
    seg_list.append(seg)

    def columns_of(which):
        found = [
            lax.dynamic_slice_in_dim(cotangent, (2 * m + which) * wcols, wcols, 1)
            for m in range(pieces)
        ]
        return found[0] if pieces == 1 else jnp.concatenate(found, 1)

    kept, sent = columns_of(side), columns_of(1 - side)
    came = swap(sent, "ctx", 1)
    flip = heads // 2
    far_kept = swap(kept, "head", flip)
    far_came = swap(came, "head", flip)
    cot_pair = jnp.stack([kept, came, far_kept, far_came], 0).reshape(2, 2, tok_rows, -1)
    offsets = [0, flip]
    flip //= 2
    while flip:
        cot_pair = jnp.concatenate([cot_pair, swap(cot_pair, "head", flip)], 0)
        offsets = offsets + [o ^ flip for o in offsets]
        flip //= 2
    cot_pair = lax.optimization_barrier(cot_pair.reshape(heads, 2 * tok_rows, -1))
    slot_of = {o: i for i, o in enumerate(offsets)}

    def cot_chunk(chunk):
        relative = (chunk // pieces) ^ head_index
        slot = jnp.zeros((), jnp.int32)
        for o, i in slot_of.items():
            slot = jnp.where(relative == o, i, slot)
        part = lax.dynamic_index_in_dim(cot_pair, slot, 0, keepdims=False)
        return lax.dynamic_slice_in_dim(part, (chunk % pieces) * wcols, wcols, 1)

    def clip(index):
        return jnp.clip(index, 0, groups - 1)

    arrivals = [(out_weight, group, True)]
    rising = falling = both = out_weight
    for s in range(1, groups):
        if s > half:
            both = shift(both, groups, (s - 1, groups), (0, groups - s))
        else:
            rising = shift(rising, groups, up=(s - 1, groups))
            falling = shift(falling, groups, down=(0, groups - s))
            both = rising + falling
        below, above = group >= s, group + s < groups
        if s < half:
            arrivals += [(rising, group - s, below), (falling, group + s, above)]
        else:
            arrivals.append((both, jnp.where(below, group - s, group + s), below | above))
    grad_both = 0.0
    for chunk, index, _ in arrivals[:-1]:
        grad_both += dot_nt(cot_chunk(clip(index)), chunk)
    grad_both = lax.optimization_barrier(grad_both)
    chunk, index, _ = arrivals[-1]
    part = cot_chunk(clip(index))[tok_rows:]
    grad_theirs = (grad_both[tok_rows:] + dot_nt(part, chunk)).astype(BF16)
    theirs = swap(grad_theirs, "ctx", 1)
    part = cot_chunk(clip(index))[:tok_rows]
    grad_mine = grad_both[:tok_rows] + dot_nt(part, chunk)

    column, row = picked_rows(table_index, level_table.shape[0])
    table = level_tables(level_table, level_column, levels, tok_bits + 1, ctx_bits, ctx_index)
    flipped = table.transpose(0, 2, 1)
    clear = (1 - (ctx_index >> jnp.arange(ctx_bits) & 1)).astype(F32)
    flags = jnp.stack([clear[0], jnp.ones((), F32), jnp.ones((), F32)])
    flags = jnp.broadcast_to(flags[:, None], (3, HD))

    def chosen_for(order):
        chosen = []
        for o in order:
            for i in range(pieces):
                chunk = (head_index ^ o) * pieces + i
                slot = jnp.zeros((), jnp.int32)
                for k, (_, index, valid) in enumerate(arrivals):
                    slot = jnp.where((chunk == index) & valid, k, slot)
                chosen.append(slot)
        return jnp.stack(chosen)

    away = [o for o in range(heads) if o & 1]
    home = [o ^ 1 for o in away]
    column, row, table, flipped, flags, away_chosen, home_chosen = lax.optimization_barrier(
        (column, row, table, flipped, flags, chosen_for(away), chosen_for(home))
    )
    near = near_of(queries, keys, values, column, table)
    attn_parts = 2
    attn_heads = head_count // attn_parts
    pairs = []
    for p in range(attn_parts):
        attn = far_of(near, queries, column, table, seg_list, levels, attn_heads, p * attn_heads)
        attn_came = swap(attn, "ctx", 1)
        pairs.append(jnp.concatenate([attn, attn_came], 0))
    attn_pair = lax.optimization_barrier(jnp.concatenate(pairs, 1))

    def weight_part(index, attn):
        return lax.dot_general(
            attn, cot_chunk(clip(index)), (((0,), (0,)), ((), ())), preferred_element_type=F32
        )

    products = []
    for s in range(1, groups + 1):
        going_up, going_down = group + groups - s, group - groups + s
        if s == groups:
            wanted = [group]
        elif s <= half:
            wanted = [jnp.where(group < half, going_up, going_down)]
        else:
            wanted = [going_up, going_down]
        found = []
        if s == 1:
            for pair in pairs:
                found.append(weight_part(wanted[0], pair))
        else:
            for index in wanted:
                product = weight_part(index, attn_pair)
                early = s <= half or s == groups
                found.append(lax.optimization_barrier(product) if early else product)
        products.append(found)
    up = down = both = None
    for s in range(1, groups):
        found = products[s - 1]
        apart = 2 * s < groups - 1
        if s == 1:
            rises = [x.astype(BF16) for x in found]
            rises = rises if apart else [jnp.concatenate(rises, 0)]
        elif s <= half:
            rises = [(found[0] + both.astype(F32)).astype(BF16)]
        else:
            rises = [(x + y.astype(F32)).astype(BF16) for x, y in zip(found, (up, down))]
        if apart:
            moved = []
            for rise in rises:
                moved.append(shift(rise, groups, (0, s - 1), (groups - s, groups)))
            both = moved[0] if len(moved) == 1 else jnp.concatenate(moved, 0)
        else:
            up = shift(rises[0], groups, up=(0, s - 1))
            down = shift(rises[-1], groups, down=(groups - s, groups))
    total = products[-1][0] + up.astype(F32) + down.astype(F32)
    grad_weight = total * (tok_rows * ctx_count) ** (-0.5)

    first, pending, grad = adjoints_of(
        queries, grad_mine, theirs, row, flipped, tok_bits + 1, ctx_bits, head_count, 0
    )
    first = swap(first, "ctx", 1, downward=True)
    adjoint = 0.0
    for bit in range(1, ctx_bits - 1):
        partner = swap(pending, "ctx", 1 << bit, downward=bit == ctx_bits - 2)
        adjoint += clear[bit] * partner[0].astype(F32)
        pending = (pending[1:].astype(F32) + partner[1:].astype(F32)).astype(BF16)
    for k in range(half):
        partner = post(pending, half, k)
        adjoint += partner[0].astype(F32)
    adjoint = adjoint.astype(BF16)[None]
    adjoint_came = swap(adjoint, "ctx", 1)
    found = [first, adjoint, adjoint_came]
    parts = 2
    part_heads = head_count // parts
    nears = ()
    for p in range(parts):
        nears = tuple(
            backward_of(
                queries, keys, values, grad, column, row, table, flipped, seg_list, levels,
                part_heads, p * part_heads, nears,
            )
        )
    grad_queries, near_dk, near_dv = nears
    grad_keys, grad_values = finish_of(
        keys, values, near_dk, near_dv, found, flags, head_count, 0, ()
    )

    sources = [chunk for chunk, _, _ in arrivals]
    sent = layer_of(away_chosen, attn_pair, sources)
    came = []
    for x in sent:
        came.append(swap(x, "head", 1))
    kept = layer_of(home_chosen, attn_pair, sources, came)
    partials = {o: [[x] for x in kept[i * pieces : (i + 1) * pieces]] for i, o in enumerate(home)}
    flip = 2
    while flip < heads:
        out_going = sorted(o for o in partials if o & flip)
        summed = {}
        for o in out_going:
            found = []
            for i in range(pieces):
                came = swap(sum_of(partials[o][i]), "head", flip)
                found.append(partials[o ^ flip][i] + [came])
            summed[o ^ flip] = found
        partials = summed
        flip *= 2
    sent = jnp.concatenate([sum_of([t[tok_rows:] for t in terms]) for terms in partials[0]], 1)
    other = swap(sent, "ctx", 1)
    columns = []
    for i, terms in enumerate(partials[0]):
        own = sum_of([t[:tok_rows] for t in terms])
        theirs = other[:, i * wcols : (i + 1) * wcols]
        columns += [jnp.where(side == 0, own, theirs), jnp.where(side == 0, theirs, own)]
    layer_out = jnp.concatenate(columns, 1)
    return (layer_out, grad_queries, grad_keys, grad_values, grad_weight)


def solution(mesh):
    placed = (
        P("ctx", "head"),
        P("ctx", "head"),
        P("ctx", "head"),
        P("ctx", "head"),
        P("head", "ctx"),
        P(None, "head", None),
        P("ctx"),
        P(),
    )
    return jax.shard_map(
        step,
        mesh=mesh,
        in_specs=placed,
        out_specs=(
            P("ctx", "head"),
            P("ctx", "head"),
            P("ctx", "head"),
            P("ctx", "head"),
            P("head", "ctx"),
        ),
        check_vma=False,
    )
```

```python
import jax
import jax.numpy as jnp
from jax import lax
from jax.experimental import pallas as pl
from jax.experimental.pallas import tpu as pltpu
from jax.sharding import PartitionSpec as P


HD = 128
F32 = jnp.float32
BF16 = jnp.bfloat16

GRANTS = {"near": 12 << 20, "far": 12 << 20, "adjoints": 12 << 20}


def route(block, axis, pairs):
    return lax.ppermute(block, axis, pairs)


def swap(block, axis, flip, upward=False, downward=False):
    pairs = [(i, i ^ flip) for i in range(lax.axis_size(axis))]
    if upward:
        pairs = [(i, j) for i, j in pairs if i < j]
    if downward:
        pairs = [(i, j) for i, j in pairs if i > j]
    return route(block, axis, pairs)


def shift(block, groups, up=None, down=None):
    pairs = []
    for step, reach in ((1, up), (-1, down)):
        if reach is None:
            continue
        for group in range(max(reach[0], 0), min(reach[1], groups - 1) + 1):
            if 0 <= group + step < groups:
                pairs += [(2 * group + side, 2 * (group + step) + side) for side in (0, 1)]
    return route(block, "ctx", pairs)


def dot_nn(a, b):
    return lax.dot_general(a, b, (((1,), (0,)), ((), ())), preferred_element_type=F32)


def dot_nt(a, b):
    return lax.dot_general(a, b, (((1,), (1,)), ((), ())), preferred_element_type=F32)


def dot_tn(a, b):
    return lax.dot_general(a, b, (((0,), (0,)), ((), ())), preferred_element_type=F32)


def post(block, source, target):
    return route(block, "ctx", [(2 * source + side, 2 * target + side) for side in (0, 1)])


def sum_of(terms):
    total = terms[0].astype(F32)
    for term in terms[1:]:
        total = total + term.astype(F32)
    return total.astype(BF16)


def halves(x):
    high = lax.reduce_precision(x, 8, 7)
    return high.astype(BF16), (x - high).astype(BF16)


def near_blocks(tok_rows):
    base = min(2 * HD, tok_rows)
    blocks = [(at, at, base, None) for at in range(0, tok_rows, base)]
    size = base
    while size < tok_rows:
        level = size.bit_length()
        blocks += [(at + size, at, size, level) for at in range(0, tok_rows, 2 * size)]
        size *= 2
    return blocks


def masks():
    row = lax.broadcasted_iota(jnp.int32, (HD, HD), 0)
    col = lax.broadcasted_iota(jnp.int32, (HD, HD), 1)
    level = jnp.zeros((HD, HD), jnp.int32)
    for bit in range(HD.bit_length() - 1):
        level = level + ((row ^ col) >= 1 << bit).astype(jnp.int32)
    return jnp.where(col <= row, level, HD - 1), level, row <= col


def tiled(tiles, flip):
    first, cross, second = tiles
    blank = jnp.zeros((HD, HD), F32)
    if flip:
        upper, lower = (first, cross), (blank, second)
    else:
        upper, lower = (first, blank), (cross, second)
    return jnp.concatenate([jnp.concatenate(upper, 1), jnp.concatenate(lower, 1)], 0)


def weight_rows(lam, row, size, level, where):
    if level is not None:
        return lam[row : row + size, level : level + 1]

    def tile(at):
        return jnp.take_along_axis(lam[at : at + HD], where[0], axis=1, mode="promise_in_bounds")

    if size == HD:
        return tile(row)
    level = HD.bit_length()
    cross = jnp.broadcast_to(lam[row + HD : row + size, level : level + 1], (HD, HD))
    return tiled((tile(row), cross, tile(row + HD)), False)


def weight_cols(lam_t, row, size, level, where):
    if level is not None:
        return lam_t[level : level + 1, row : row + size]

    def tile(at):
        found = [
            jnp.take_along_axis(
                lam_t[:8, at : at + HD], where[1][i : i + 8], axis=0, mode="promise_in_bounds"
            )
            for i in range(0, HD, 8)
        ]
        return jnp.where(where[2], jnp.concatenate(found, 0), 0.0)

    if size == HD:
        return tile(row)
    level = HD.bit_length()
    cross = jnp.broadcast_to(lam_t[level : level + 1, row + HD : row + size], (HD, HD))
    return tiled((tile(row), cross, tile(row + HD)), True)


def add_rows(total, at, part):
    for i in range(0, part.shape[0], HD):
        slot = (at + i) // HD
        piece = part[i : i + HD]
        total[slot] = piece if total[slot] is None else total[slot] + piece


def state_kernel(pack, k_ref, v_ref, o_ref):
    for n in range(pack):
        at = pl.ds(n * HD, HD)
        o_ref[n] = dot_tn(k_ref[:, at], v_ref[:, at]).astype(BF16)


def near_kernel(pack, q_ref, k_ref, v_ref, picked_ref, table_ref, o_ref):
    tok_rows = q_ref.shape[0]
    where = masks()
    for n in range(pack):
        q, k, v = (ref[:, pl.ds(n * HD, HD)] for ref in (q_ref, k_ref, v_ref))
        lam = dot_nn(picked_ref[...], table_ref[n])
        total = [None] * (tok_rows // HD)
        for row, col, size, level in near_blocks(tok_rows):
            weight = weight_rows(lam, row, size, level, where)
            score = dot_nt(q[row : row + size], k[col : col + size])
            add_rows(total, row, dot_nn((weight * score).astype(BF16), v[col : col + size]))
        for i in range(tok_rows // HD):
            o_ref[i * HD : (i + 1) * HD, pl.ds(n * HD, HD)] = total[i]


def far_kernel(pack, far, levels, near_ref, q_ref, picked_ref, table_ref, *refs):
    segs, o_ref = refs[:far], refs[far]
    for n in range(pack):
        lanes = pl.ds(n * HD, HD)
        lam = dot_nn(picked_ref[...], table_ref[n])
        through = dot_nn(q_ref[:, lanes], jnp.concatenate([seg[n] for seg in segs], 1))
        out = near_ref[:, lanes]
        for j in range(far):
            out = out + lam[:, levels + j : levels + j + 1] * through[:, j * HD : (j + 1) * HD]
        o_ref[:, lanes] = out.astype(BF16)


def adjoint_kernel(
    pack, far, near, picked_ref, q_ref, mine_ref, theirs_ref, table_ref, first_ref, rest_ref, g_ref
):
    for n in range(pack):
        lanes = pl.ds(n * HD, HD)
        g = (mine_ref[:, lanes] + theirs_ref[:, lanes].astype(F32)).astype(BF16)
        g_ref[:, lanes] = g
        lam = dot_nn(table_ref[n], picked_ref[...])
        q_t = q_ref[:, lanes].T.astype(F32)
        stacked = jnp.concatenate(
            [(lam[near + j : near + j + 1] * q_t).astype(BF16) for j in range(far)], 0
        )
        found = dot_nn(stacked, g)
        first_ref[0, n] = found[:HD].astype(BF16)
        for j in range(1, far):
            rest_ref[j - 1, n] = found[j * HD : (j + 1) * HD].astype(BF16)


def backward_kernel(
    pack, far, levels, q_ref, k_ref, v_ref, g_ref, column_ref, row_ref, table_ref, flipped_ref, *refs
):
    segs, (dq_ref, dk_ref, dv_ref) = refs[:far], refs[far:]
    tok_rows = q_ref.shape[0]
    where = masks()
    for n in range(pack):
        lanes = pl.ds(n * HD, HD)
        q_all, k_all, v_all, g_all = (ref[:, lanes] for ref in (q_ref, k_ref, v_ref, g_ref))
        lam = dot_nn(column_ref[...], table_ref[n])
        lam_t = dot_nn(flipped_ref[n], row_ref[...])
        dq, dk, dv = ([None] * (tok_rows // HD) for _ in range(3))
        for row, col, size, level in near_blocks(tok_rows):
            q, g = q_all[row : row + size], g_all[row : row + size]
            k, v = k_all[col : col + size], v_all[col : col + size]
            weight = weight_rows(lam, row, size, level, where)
            flipped = weight_cols(lam_t, row, size, level, where)
            add_rows(dq, row, dot_nn((weight * dot_nt(g, v)).astype(BF16), k))
            add_rows(dk, col, dot_nn((flipped * dot_nt(v, g)).astype(BF16), q))
            add_rows(dv, col, dot_nn((flipped * dot_nt(k, q)).astype(BF16), g))
        back = dot_nt(g_all, jnp.concatenate([seg[n] for seg in segs], 0))
        for i in range(tok_rows // HD):
            out = dq[i]
            at = i * HD
            for j in range(far):
                scale = lam[at : at + HD, levels + j : levels + j + 1]
                out = out + scale * back[at : at + HD, j * HD : (j + 1) * HD]
            dq_ref[at : at + HD, lanes] = out.astype(BF16)
            dk_ref[at : at + HD, lanes] = dk[i].astype(BF16)
            dv_ref[at : at + HD, lanes] = dv[i].astype(BF16)


def finish_kernel(pack, far, clear_ref, k_ref, v_ref, dk_ref, dv_ref, *refs):
    found, (dk_out, dv_out) = refs[:far], refs[far:]
    for n in range(pack):
        lanes = pl.ds(n * HD, HD)
        adjoint = clear_ref[0:1] * found[0][0, n].astype(F32)
        for j in range(1, far):
            adjoint = adjoint + clear_ref[j : j + 1] * found[j][0, n].astype(F32)
        adjoint = adjoint.astype(BF16)
        dk_out[:, lanes] = (dk_ref[:, lanes].astype(F32) + dot_nt(v_ref[:, lanes], adjoint)).astype(BF16)
        dv_out[:, lanes] = (dv_ref[:, lanes].astype(F32) + dot_nn(k_ref[:, lanes], adjoint)).astype(BF16)


def shape(dims, kind):
    return jax.ShapeDtypeStruct(dims, kind)


def per_head(name, kernel, most, flops, heads, first, ins, outs, consts=(), into=()):
    pack = min(most, heads)

    def spec(x):
        if len(x.shape) == 2:
            at = first // pack if x.shape[1] > heads * HD else 0
            return pl.BlockSpec((ins[0].shape[0], pack * HD), lambda h: (0, h + at))
        at = first // pack if x.shape[-3] > heads else 0
        lead = (0,) * (len(x.shape) - 3)
        return pl.BlockSpec(x.shape[:-3] + (pack,) + x.shape[-2:], lambda h: lead + (h + at, 0, 0))

    def run(*refs):
        kernel(pack, *refs[len(into) :])

    size = flops // HD + sum(x.size * x.dtype.itemsize for x in outs)
    whole = [pl.BlockSpec(x.shape, lambda h: (0, 0)) for x in consts]
    kept = [pl.BlockSpec(memory_space=pl.ANY)] * len(into)
    single = len(outs) == 1
    return pl.pallas_call(
        run,
        grid=(heads // pack,),
        in_specs=kept + whole + [spec(x) for x in ins],
        out_specs=spec(outs[0]) if single else [spec(x) for x in outs],
        out_shape=outs[0] if single else list(outs),
        input_output_aliases={i: i for i in range(len(into))},
        compiler_params=pltpu.CompilerParams(vmem_limit_bytes=GRANTS.get(name)),
        cost_estimate=pl.CostEstimate(flops=flops, bytes_accessed=size, transcendentals=0),
    )(*into, *consts, *ins)


def states_of(keys, values):
    rows, width = keys.shape
    heads = width // HD
    return per_head(
        "states", state_kernel, 4, 2 * rows * width * HD, heads, 0,
        (keys, values), (shape((heads, HD, HD), BF16),),
    )


def near_of(queries, keys, values, column, table):
    rows, width = queries.shape

    def kernel(pack, picked, q, k, v, table, out):
        near_kernel(pack, q, k, v, picked, table, out)

    return per_head(
        "near", kernel, 2, 6 * rows * rows * width, width // HD, 0,
        (queries, keys, values, table), (shape((rows, width), F32),), (column,),
    )


def far_of(near, queries, column, table, segs, levels, heads, first):
    rows = queries.shape[0]

    def kernel(pack, picked, *refs):
        far_kernel(pack, len(segs), levels, *refs[:2], picked, *refs[2:])

    return per_head(
        "far", kernel, 2, 2 * len(segs) * rows * heads * HD * HD, heads, first,
        (near, queries, table, *segs), (shape((rows, heads * HD), BF16),), (column,),
    )


def adjoints_of(queries, mine, theirs, row, flipped, near, far, heads, first):
    rows = queries.shape[0]

    def kernel(pack, *refs):
        adjoint_kernel(pack, far, near, *refs)

    return per_head(
        "adjoints", kernel, 4, 2 * far * rows * heads * HD * HD, heads, first,
        (queries, mine, theirs, flipped),
        (
            shape((1, heads, HD, HD), BF16),
            shape((far - 1, heads, HD, HD), BF16),
            shape((rows, heads * HD), BF16),
        ),
        (row,),
    )


def backward_of(queries, keys, values, grad, column, row, table, flipped, segs, levels, heads, first, into):
    rows, width = queries.shape

    def kernel(pack, column, row, *refs):
        backward_kernel(pack, len(segs), levels, *refs[:4], column, row, *refs[4:])

    part = shape((rows, width), BF16)
    return per_head(
        "retreat", kernel, 2, 12 * rows * rows * heads * HD, heads, first,
        (queries, keys, values, grad, table, flipped, *segs),
        (shape((rows, width), BF16), part, part), (column, row), into,
    )


def finish_of(keys, values, dk, dv, found, clear, heads, first, into):
    rows, width = keys.shape

    def kernel(pack, *refs):
        finish_kernel(pack, len(found), *refs)

    return per_head(
        "finish", kernel, 4, 4 * rows * heads * HD * HD, heads, first,
        (keys, values, dk, dv, *found), (shape((rows, width), BF16),) * 2, (clear,), into,
    )


def blank(dims):
    return pl.pallas_call(
        lambda o_ref: None,
        out_specs=pl.BlockSpec(memory_space=pl.ANY),
        out_shape=shape(dims, BF16),
        name="blank",
    )()


def level_scales(levels):
    level_ids = jnp.arange(levels, dtype=jnp.float32)
    return jnp.where(level_ids < 0.5, 1.0, jnp.exp2(-(level_ids - 1.0) * 0.5))


def level_tables(level_table, level_column, levels, near, ctx_bits, ctx_index):
    columns = (
        level_column[:levels, None] == jnp.arange(level_table.shape[2], dtype=jnp.int32)[None, :]
    ).astype(F32)
    scaled = columns * (level_scales(levels) * HD ** (-0.5))[:, None]
    bits = (ctx_index >> jnp.arange(ctx_bits, dtype=jnp.int32) & 1).astype(F32)
    scaled = jnp.concatenate([scaled, scaled[near:] * bits[:, None]], 0)
    table = jnp.sum(level_table.transpose(1, 0, 2)[:, :, None, :] * scaled[None, None], -1)
    table = jnp.pad(table, ((0, 0), (0, 0), (0, HD - table.shape[2])))
    high, low = halves(table)
    return jnp.concatenate([high, low], 1)


def picked_rows(table_index, table_count):
    ids = jnp.arange(2 * table_count, dtype=jnp.int32) % table_count
    column = (table_index[:, None] == ids[None, :]).astype(BF16)
    row = (table_index[None, :] == ids[:, None]).astype(BF16)
    return column, row


def step(queries, keys, values, cotangent, out_weight, level_table, table_index, level_column):
    tok_rows, feature_width = queries.shape
    head_count = feature_width // HD
    ctx_count = lax.axis_size("ctx")
    ctx_bits = ctx_count.bit_length() - 1
    tok_bits = tok_rows.bit_length() - 1
    levels = tok_bits + ctx_bits + 1
    ctx_index = lax.axis_index("ctx")
    head_index = lax.axis_index("head")
    heads = lax.axis_size("head")
    groups = ctx_count // 2
    half = groups // 2
    side = ctx_index & 1
    group = ctx_index >> 1
    wcols = out_weight.shape[1]
    pieces = feature_width // wcols // 2

    running = states_of(keys, values)
    seg_list = []
    for bit in range(ctx_bits - 1):
        seg = swap(running, "ctx", 1 << bit, upward=0 < bit == ctx_bits - 2)
        seg_list.append(seg)
        running = (running.astype(F32) + seg.astype(F32)).astype(BF16)
    seg = None
    for k in range(half):
        sent = post(running, half - 1, groups - 1 - k)
        seg = sent if seg is None else seg + sent
    seg_list.append(seg)

    def columns_of(which):
        found = [
            lax.dynamic_slice_in_dim(cotangent, (2 * m + which) * wcols, wcols, 1)
            for m in range(pieces)
        ]
        return found[0] if pieces == 1 else jnp.concatenate(found, 1)

    kept, sent = columns_of(side), columns_of(1 - side)
    came = swap(sent, "ctx", 1)
    flip = heads // 2
    far_kept = swap(kept, "head", flip)
    far_came = swap(came, "head", flip)
    cot_pair = jnp.stack([kept, came, far_kept, far_came], 0).reshape(2, 2, tok_rows, -1)
    offsets = [0, flip]
    flip //= 2
    while flip:
        cot_pair = jnp.concatenate([cot_pair, swap(cot_pair, "head", flip)], 0)
        offsets = offsets + [o ^ flip for o in offsets]
        flip //= 2
    cot_pair = lax.optimization_barrier(cot_pair.reshape(heads, 2 * tok_rows, -1))
    slot_of = {o: i for i, o in enumerate(offsets)}

    def cot_chunk(chunk):
        relative = (chunk // pieces) ^ head_index
        slot = jnp.zeros((), jnp.int32)
        for o, i in slot_of.items():
            slot = jnp.where(relative == o, i, slot)
        part = lax.dynamic_index_in_dim(cot_pair, slot, 0, keepdims=False)
        return lax.dynamic_slice_in_dim(part, (chunk % pieces) * wcols, wcols, 1)

    def clip(index):
        return jnp.clip(index, 0, groups - 1)

    arrivals = [(out_weight, group, True)]
    rising = falling = both = out_weight
    for s in range(1, groups):
        if s > half:
            both = shift(both, groups, (s - 1, groups), (0, groups - s))
        else:
            rising = shift(rising, groups, up=(s - 1, groups))
            falling = shift(falling, groups, down=(0, groups - s))
            both = rising + falling
        below, above = group >= s, group + s < groups
        if s < half:
            arrivals += [(rising, group - s, below), (falling, group + s, above)]
        else:
            arrivals.append((both, jnp.where(below, group - s, group + s), below | above))
    all_weight = blank((groups + 1,) + out_weight.shape)
    for chunk, index, valid in arrivals:
        place = jnp.where(valid, index, groups)
        all_weight = lax.dynamic_update_index_in_dim(all_weight, chunk, place, 0)

    grad_both = 0.0
    for chunk, index, _ in arrivals[:-1]:
        grad_both += dot_nt(cot_chunk(clip(index)), chunk)
    grad_both = lax.optimization_barrier(grad_both)
    chunk, index, _ = arrivals[-1]
    part = cot_chunk(clip(index))[tok_rows:]
    grad_theirs = (grad_both[tok_rows:] + dot_nt(part, chunk)).astype(BF16)
    theirs = swap(grad_theirs, "ctx", 1)
    part = cot_chunk(clip(index))[:tok_rows]
    grad_mine = grad_both[:tok_rows] + dot_nt(part, chunk)

    column, row = picked_rows(table_index, level_table.shape[0])
    table = level_tables(level_table, level_column, levels, tok_bits + 1, ctx_bits, ctx_index)
    flipped = table.transpose(0, 2, 1)
    clear = (1 - (ctx_index >> jnp.arange(ctx_bits) & 1)).astype(F32)
    flags = jnp.stack([clear[0], jnp.ones((), F32), jnp.ones((), F32)])
    flags = jnp.broadcast_to(flags[:, None], (3, HD))

    away = [o for o in range(heads) if o & 1]
    home = [o ^ 1 for o in away]
    column, row, table, flipped, flags = lax.optimization_barrier(
        (column, row, table, flipped, flags)
    )
    near = near_of(queries, keys, values, column, table)
    attn_parts = 2
    attn_heads = head_count // attn_parts
    pairs = []
    for p in range(attn_parts):
        attn = far_of(near, queries, column, table, seg_list, levels, attn_heads, p * attn_heads)
        attn_came = swap(attn, "ctx", 1)
        pairs.append(jnp.concatenate([attn, attn_came], 0))
    attn_pair = lax.optimization_barrier(jnp.concatenate(pairs, 1))

    def weight_part(index, attn):
        return lax.dot_general(
            attn, cot_chunk(clip(index)), (((0,), (0,)), ((), ())), preferred_element_type=F32
        )

    products = []
    for s in range(1, groups + 1):
        going_up, going_down = group + groups - s, group - groups + s
        if s == groups:
            wanted = [group]
        elif s <= half:
            wanted = [jnp.where(group < half, going_up, going_down)]
        else:
            wanted = [going_up, going_down]
        found = []
        if s == 1:
            for pair in pairs:
                found.append(weight_part(wanted[0], pair))
        else:
            for index in wanted:
                product = weight_part(index, attn_pair).astype(BF16)
                found.append(lax.optimization_barrier(product).astype(F32))
        products.append(found)
    up = down = both = None
    for s in range(1, groups):
        found = products[s - 1]
        apart = 2 * s < groups - 1
        if s == 1:
            rises = [x.astype(BF16) for x in found]
            rises = rises if apart else [jnp.concatenate(rises, 0)]
        elif s <= half:
            rises = [(found[0] + both.astype(F32)).astype(BF16)]
        else:
            rises = [(x + y.astype(F32)).astype(BF16) for x, y in zip(found, (up, down))]
        if apart:
            moved = []
            for rise in rises:
                moved.append(shift(rise, groups, (0, s - 1), (groups - s, groups)))
            both = moved[0] if len(moved) == 1 else jnp.concatenate(moved, 0)
        else:
            up = shift(rises[0], groups, up=(0, s - 1))
            down = shift(rises[-1], groups, down=(groups - s, groups))
    total = products[-1][0] + up.astype(F32) + down.astype(F32)
    grad_weight = total * (tok_rows * ctx_count) ** (-0.5)

    first, pending, grad = adjoints_of(
        queries, grad_mine, theirs, row, flipped, tok_bits + 1, ctx_bits, head_count, 0
    )
    first = swap(first, "ctx", 1, downward=True)
    adjoint = 0.0
    for bit in range(1, ctx_bits - 1):
        partner = swap(pending, "ctx", 1 << bit, downward=bit == ctx_bits - 2)
        adjoint += clear[bit] * partner[0].astype(F32)
        pending = (pending[1:].astype(F32) + partner[1:].astype(F32)).astype(BF16)
    for k in range(half):
        partner = post(pending, half, k)
        adjoint += partner[0].astype(F32)
    adjoint = adjoint.astype(BF16)[None]
    adjoint_came = swap(adjoint, "ctx", 1)
    found = [first, adjoint, adjoint_came]
    parts = 2
    part_heads = head_count // parts
    nears = ()
    for p in range(parts):
        nears = tuple(
            backward_of(
                queries, keys, values, grad, column, row, table, flipped, seg_list, levels,
                part_heads, p * part_heads, nears,
            )
        )
    grad_queries, near_dk, near_dv = nears
    grad_keys, grad_values = finish_of(
        keys, values, near_dk, near_dv, found, flags, head_count, 0, ()
    )

    def layer_part(offset, i):
        chunk = (head_index ^ offset) * pieces + i
        weight = lax.dynamic_index_in_dim(all_weight, chunk, 0, keepdims=False)
        return dot_nn(attn_pair, weight)

    came = {}
    for o in away:
        for i in range(pieces):
            sent = layer_part(o, i).astype(BF16)
            came[o ^ 1, i] = swap(sent, "head", 1)
    kept = []
    for o in home:
        for i in range(pieces):
            kept.append((layer_part(o, i) + came[o, i].astype(F32)).astype(BF16))
    partials = {o: [[x] for x in kept[i * pieces : (i + 1) * pieces]] for i, o in enumerate(home)}
    flip = 2
    while flip < heads:
        out_going = sorted(o for o in partials if o & flip)
        summed = {}
        for o in out_going:
            found = []
            for i in range(pieces):
                came = swap(sum_of(partials[o][i]), "head", flip)
                found.append(partials[o ^ flip][i] + [came])
            summed[o ^ flip] = found
        partials = summed
        flip *= 2
    sent = jnp.concatenate([sum_of([t[tok_rows:] for t in terms]) for terms in partials[0]], 1)
    other = swap(sent, "ctx", 1)
    columns = []
    for i, terms in enumerate(partials[0]):
        own = sum_of([t[:tok_rows] for t in terms])
        theirs = other[:, i * wcols : (i + 1) * wcols]
        columns += [jnp.where(side == 0, own, theirs), jnp.where(side == 0, theirs, own)]
    layer_out = jnp.concatenate(columns, 1)
    return (layer_out, grad_queries, grad_keys, grad_values, grad_weight)


def solution(mesh):
    placed = (
        P("ctx", "head"),
        P("ctx", "head"),
        P("ctx", "head"),
        P("ctx", "head"),
        P("head", "ctx"),
        P(None, "head", None),
        P("ctx"),
        P(),
    )
    return jax.shard_map(
        step,
        mesh=mesh,
        in_specs=placed,
        out_specs=(
            P("ctx", "head"),
            P("ctx", "head"),
            P("ctx", "head"),
            P("ctx", "head"),
            P("head", "ctx"),
        ),
        check_vma=False,
    )
```

```python
import jax
import jax.numpy as jnp
from jax import lax
from jax.experimental import pallas as pl
from jax.experimental.pallas import tpu as pltpu
from jax.sharding import PartitionSpec as P


HD = 128
F32 = jnp.float32
BF16 = jnp.bfloat16

GRANTS = {"near": 12 << 20, "far": 12 << 20, "adjoints": 12 << 20}


def route(block, axis, pairs):
    return lax.ppermute(block, axis, pairs)


def swap(block, axis, flip, upward=False, downward=False, within=0):
    pairs = [(i, i ^ flip) for i in range(lax.axis_size(axis)) if i & within == within]
    if upward:
        pairs = [(i, j) for i, j in pairs if i < j]
    if downward:
        pairs = [(i, j) for i, j in pairs if i > j]
    return route(block, axis, pairs)


def shift(block, groups, up=None, down=None):
    pairs = []
    for step, reach in ((1, up), (-1, down)):
        if reach is None:
            continue
        for group in range(max(reach[0], 0), min(reach[1], groups - 1) + 1):
            if 0 <= group + step < groups:
                pairs += [(2 * group + side, 2 * (group + step) + side) for side in (0, 1)]
    return route(block, "ctx", pairs)


def dot_nn(a, b):
    return lax.dot_general(a, b, (((1,), (0,)), ((), ())), preferred_element_type=F32)


def dot_nt(a, b):
    return lax.dot_general(a, b, (((1,), (1,)), ((), ())), preferred_element_type=F32)


def dot_tn(a, b):
    return lax.dot_general(a, b, (((0,), (0,)), ((), ())), preferred_element_type=F32)


def post(block, source, target):
    return route(block, "ctx", [(2 * source + side, 2 * target + side) for side in (0, 1)])


def sum_of(terms):
    total = terms[0].astype(F32)
    for term in terms[1:]:
        total = total + term.astype(F32)
    return total.astype(BF16)


def halves(x):
    high = lax.reduce_precision(x, 8, 7)
    return high.astype(BF16), (x - high).astype(BF16)


def near_blocks(tok_rows):
    base = min(2 * HD, tok_rows)
    blocks = [(at, at, base, None) for at in range(0, tok_rows, base)]
    size = base
    while size < tok_rows:
        level = size.bit_length()
        blocks += [(at + size, at, size, level) for at in range(0, tok_rows, 2 * size)]
        size *= 2
    return blocks


def masks():
    row = lax.broadcasted_iota(jnp.int32, (HD, HD), 0)
    col = lax.broadcasted_iota(jnp.int32, (HD, HD), 1)
    level = jnp.zeros((HD, HD), jnp.int32)
    for bit in range(HD.bit_length() - 1):
        level = level + ((row ^ col) >= 1 << bit).astype(jnp.int32)
    return jnp.where(col <= row, level, HD - 1), level, row <= col


def tiled(tiles, flip):
    first, cross, second = tiles
    blank = jnp.zeros((HD, HD), F32)
    if flip:
        upper, lower = (first, cross), (blank, second)
    else:
        upper, lower = (first, blank), (cross, second)
    return jnp.concatenate([jnp.concatenate(upper, 1), jnp.concatenate(lower, 1)], 0)


def weight_rows(lam, row, size, level, where):
    if level is not None:
        return lam[row : row + size, level : level + 1]

    def tile(at):
        return jnp.take_along_axis(lam[at : at + HD], where[0], axis=1, mode="promise_in_bounds")

    if size == HD:
        return tile(row)
    level = HD.bit_length()
    cross = jnp.broadcast_to(lam[row + HD : row + size, level : level + 1], (HD, HD))
    return tiled((tile(row), cross, tile(row + HD)), False)


def weight_cols(lam_t, row, size, level, where):
    if level is not None:
        return lam_t[level : level + 1, row : row + size]

    def tile(at):
        found = [
            jnp.take_along_axis(
                lam_t[:8, at : at + HD], where[1][i : i + 8], axis=0, mode="promise_in_bounds"
            )
            for i in range(0, HD, 8)
        ]
        return jnp.where(where[2], jnp.concatenate(found, 0), 0.0)

    if size == HD:
        return tile(row)
    level = HD.bit_length()
    cross = jnp.broadcast_to(lam_t[level : level + 1, row + HD : row + size], (HD, HD))
    return tiled((tile(row), cross, tile(row + HD)), True)


def add_rows(total, at, part):
    for i in range(0, part.shape[0], HD):
        slot = (at + i) // HD
        piece = part[i : i + HD]
        total[slot] = piece if total[slot] is None else total[slot] + piece


def state_kernel(pack, k_ref, v_ref, o_ref):
    for n in range(pack):
        at = pl.ds(n * HD, HD)
        o_ref[n] = dot_tn(k_ref[:, at], v_ref[:, at]).astype(BF16)


def near_kernel(pack, q_ref, k_ref, v_ref, picked_ref, table_ref, o_ref):
    tok_rows = q_ref.shape[0]
    where = masks()
    for n in range(pack):
        q, k, v = (ref[:, pl.ds(n * HD, HD)] for ref in (q_ref, k_ref, v_ref))
        lam = dot_nn(picked_ref[...], table_ref[n])
        total = [None] * (tok_rows // HD)
        for row, col, size, level in near_blocks(tok_rows):
            weight = weight_rows(lam, row, size, level, where)
            score = dot_nt(q[row : row + size], k[col : col + size])
            add_rows(total, row, dot_nn((weight * score).astype(BF16), v[col : col + size]))
        for i in range(tok_rows // HD):
            o_ref[i * HD : (i + 1) * HD, pl.ds(n * HD, HD)] = total[i]


def far_kernel(pack, far, levels, near_ref, q_ref, picked_ref, table_ref, *refs):
    segs, o_ref = refs[:far], refs[far]
    for n in range(pack):
        lanes = pl.ds(n * HD, HD)
        lam = dot_nn(picked_ref[...], table_ref[n])
        through = dot_nn(q_ref[:, lanes], jnp.concatenate([seg[n] for seg in segs], 1))
        out = near_ref[:, lanes]
        for j in range(far):
            out = out + lam[:, levels + j : levels + j + 1] * through[:, j * HD : (j + 1) * HD]
        o_ref[:, lanes] = out.astype(BF16)


def adjoint_kernel(
    pack, far, near, picked_ref, q_ref, mine_ref, theirs_ref, table_ref, *refs
):
    level_refs, g_ref = refs[:far], refs[far]
    for n in range(pack):
        lanes = pl.ds(n * HD, HD)
        g = (mine_ref[:, lanes] + theirs_ref[:, lanes].astype(F32)).astype(BF16)
        g_ref[:, lanes] = g
        lam = dot_nn(table_ref[n], picked_ref[...])
        q_t = q_ref[:, lanes].T.astype(F32)
        stacked = jnp.concatenate(
            [(lam[near + j : near + j + 1] * q_t).astype(BF16) for j in range(far)], 0
        )
        found = dot_nn(stacked, g)
        for j in range(far):
            level_refs[j][n] = found[j * HD : (j + 1) * HD].astype(BF16)


def backward_kernel(
    pack, far, levels, q_ref, k_ref, v_ref, g_ref, column_ref, row_ref, table_ref, flipped_ref, *refs
):
    segs, (dq_ref, dk_ref, dv_ref) = refs[:far], refs[far:]
    tok_rows = q_ref.shape[0]
    where = masks()
    for n in range(pack):
        lanes = pl.ds(n * HD, HD)
        q_all, k_all, v_all, g_all = (ref[:, lanes] for ref in (q_ref, k_ref, v_ref, g_ref))
        lam = dot_nn(column_ref[...], table_ref[n])
        lam_t = dot_nn(flipped_ref[n], row_ref[...])
        dq, dk, dv = ([None] * (tok_rows // HD) for _ in range(3))
        for row, col, size, level in near_blocks(tok_rows):
            q, g = q_all[row : row + size], g_all[row : row + size]
            k, v = k_all[col : col + size], v_all[col : col + size]
            weight = weight_rows(lam, row, size, level, where)
            flipped = weight_cols(lam_t, row, size, level, where)
            add_rows(dq, row, dot_nn((weight * dot_nt(g, v)).astype(BF16), k))
            add_rows(dk, col, dot_nn((flipped * dot_nt(v, g)).astype(BF16), q))
            add_rows(dv, col, dot_nn((flipped * dot_nt(k, q)).astype(BF16), g))
        back = dot_nt(g_all, jnp.concatenate([seg[n] for seg in segs], 0))
        for i in range(tok_rows // HD):
            out = dq[i]
            at = i * HD
            for j in range(far):
                scale = lam[at : at + HD, levels + j : levels + j + 1]
                out = out + scale * back[at : at + HD, j * HD : (j + 1) * HD]
            dq_ref[at : at + HD, lanes] = out.astype(BF16)
            dk_ref[at : at + HD, lanes] = dk[i].astype(BF16)
            dv_ref[at : at + HD, lanes] = dv[i].astype(BF16)


def finish_kernel(pack, far, clear_ref, k_ref, v_ref, dk_ref, dv_ref, *refs):
    found, (dk_out, dv_out) = refs[:far], refs[far:]
    for n in range(pack):
        lanes = pl.ds(n * HD, HD)
        adjoint = clear_ref[0:1] * found[0][n].astype(F32)
        for j in range(1, far):
            adjoint = adjoint + clear_ref[j : j + 1] * found[j][n].astype(F32)
        adjoint = adjoint.astype(BF16)
        dk_out[:, lanes] = (dk_ref[:, lanes].astype(F32) + dot_nt(v_ref[:, lanes], adjoint)).astype(BF16)
        dv_out[:, lanes] = (dv_ref[:, lanes].astype(F32) + dot_nn(k_ref[:, lanes], adjoint)).astype(BF16)


def shape(dims, kind):
    return jax.ShapeDtypeStruct(dims, kind)


def per_head(name, kernel, most, flops, heads, first, ins, outs, consts=(), into=()):
    pack = min(most, heads)

    def spec(x):
        if len(x.shape) == 2:
            at = first // pack if x.shape[1] > heads * HD else 0
            return pl.BlockSpec((ins[0].shape[0], pack * HD), lambda h: (0, h + at))
        at = first // pack if x.shape[-3] > heads else 0
        lead = (0,) * (len(x.shape) - 3)
        return pl.BlockSpec(x.shape[:-3] + (pack,) + x.shape[-2:], lambda h: lead + (h + at, 0, 0))

    def run(*refs):
        kernel(pack, *refs[len(into) :])

    size = flops // HD + sum(x.size * x.dtype.itemsize for x in outs)
    whole = [pl.BlockSpec(x.shape, lambda h: (0, 0)) for x in consts]
    kept = [pl.BlockSpec(memory_space=pl.ANY)] * len(into)
    single = len(outs) == 1
    return pl.pallas_call(
        run,
        grid=(heads // pack,),
        in_specs=kept + whole + [spec(x) for x in ins],
        out_specs=spec(outs[0]) if single else [spec(x) for x in outs],
        out_shape=outs[0] if single else list(outs),
        input_output_aliases={i: i for i in range(len(into))},
        compiler_params=pltpu.CompilerParams(vmem_limit_bytes=GRANTS.get(name)),
        cost_estimate=pl.CostEstimate(flops=flops, bytes_accessed=size, transcendentals=0),
    )(*into, *consts, *ins)


def states_of(keys, values):
    rows, width = keys.shape
    heads = width // HD
    return per_head(
        "states", state_kernel, 4, 2 * rows * width * HD, heads, 0,
        (keys, values), (shape((heads, HD, HD), BF16),),
    )


def near_of(queries, keys, values, column, table):
    rows, width = queries.shape

    def kernel(pack, picked, q, k, v, table, out):
        near_kernel(pack, q, k, v, picked, table, out)

    return per_head(
        "near", kernel, 2, 6 * rows * rows * width, width // HD, 0,
        (queries, keys, values, table), (shape((rows, width), F32),), (column,),
    )


def far_of(near, queries, column, table, segs, levels, heads, first):
    rows = queries.shape[0]

    def kernel(pack, picked, *refs):
        far_kernel(pack, len(segs), levels, *refs[:2], picked, *refs[2:])

    return per_head(
        "far", kernel, 2, 2 * len(segs) * rows * heads * HD * HD, heads, first,
        (near, queries, table, *segs), (shape((rows, heads * HD), BF16),), (column,),
    )


def adjoints_of(queries, mine, theirs, row, flipped, near, far, heads, first):
    rows = queries.shape[0]

    def kernel(pack, *refs):
        adjoint_kernel(pack, far, near, *refs)

    return per_head(
        "adjoints", kernel, 4, 2 * far * rows * heads * HD * HD, heads, first,
        (queries, mine, theirs, flipped),
        (shape((heads, HD, HD), BF16),) * far + (shape((rows, heads * HD), BF16),),
        (row,),
    )


def backward_of(queries, keys, values, grad, column, row, table, flipped, segs, levels, heads, first, into):
    rows, width = queries.shape

    def kernel(pack, column, row, *refs):
        backward_kernel(pack, len(segs), levels, *refs[:4], column, row, *refs[4:])

    part = shape((rows, width), BF16)
    return per_head(
        "retreat", kernel, 2, 12 * rows * rows * heads * HD, heads, first,
        (queries, keys, values, grad, table, flipped, *segs),
        (shape((rows, width), BF16), part, part), (column, row), into,
    )


def finish_of(keys, values, dk, dv, found, clear, heads, first, into):
    rows, width = keys.shape

    def kernel(pack, *refs):
        finish_kernel(pack, len(found), *refs)

    return per_head(
        "finish", kernel, 4, 4 * rows * heads * HD * HD, heads, first,
        (keys, values, dk, dv, *found), (shape((rows, width), BF16),) * 2, (clear,), into,
    )


def blank(dims):
    return pl.pallas_call(
        lambda o_ref: None,
        out_specs=pl.BlockSpec(memory_space=pl.ANY),
        out_shape=shape(dims, BF16),
        name="blank",
    )()


def level_scales(levels):
    level_ids = jnp.arange(levels, dtype=jnp.float32)
    return jnp.where(level_ids < 0.5, 1.0, jnp.exp2(-(level_ids - 1.0) * 0.5))


def level_tables(level_table, level_column, levels, near, ctx_bits, ctx_index):
    columns = (
        level_column[:levels, None] == jnp.arange(level_table.shape[2], dtype=jnp.int32)[None, :]
    ).astype(F32)
    scaled = columns * (level_scales(levels) * HD ** (-0.5))[:, None]
    bits = (ctx_index >> jnp.arange(ctx_bits, dtype=jnp.int32) & 1).astype(F32)
    scaled = jnp.concatenate([scaled, scaled[near:] * bits[:, None]], 0)
    table = jnp.sum(level_table.transpose(1, 0, 2)[:, :, None, :] * scaled[None, None], -1)
    table = jnp.pad(table, ((0, 0), (0, 0), (0, HD - table.shape[2])))
    high, low = halves(table)
    return jnp.concatenate([high, low], 1)


def picked_rows(table_index, table_count):
    ids = jnp.arange(2 * table_count, dtype=jnp.int32) % table_count
    column = (table_index[:, None] == ids[None, :]).astype(BF16)
    row = (table_index[None, :] == ids[:, None]).astype(BF16)
    return column, row


def step(queries, keys, values, cotangent, out_weight, level_table, table_index, level_column):
    tok_rows, feature_width = queries.shape
    head_count = feature_width // HD
    ctx_count = lax.axis_size("ctx")
    ctx_bits = ctx_count.bit_length() - 1
    tok_bits = tok_rows.bit_length() - 1
    levels = tok_bits + ctx_bits + 1
    ctx_index = lax.axis_index("ctx")
    head_index = lax.axis_index("head")
    heads = lax.axis_size("head")
    groups = ctx_count // 2
    half = groups // 2
    side = ctx_index & 1
    group = ctx_index >> 1
    wcols = out_weight.shape[1]
    pieces = feature_width // wcols // 2

    running = states_of(keys, values)
    seg_list = []
    for bit in range(ctx_bits - 1):
        seg = swap(running, "ctx", 1 << bit, upward=0 < bit == ctx_bits - 2)
        seg_list.append(seg)
        running = (running.astype(F32) + seg.astype(F32)).astype(BF16)
    seg = None
    for k in range(half):
        sent = post(running, half - 1, groups - 1 - k)
        seg = sent if seg is None else seg + sent
    seg_list.append(seg)

    def columns_of(which):
        found = [
            lax.dynamic_slice_in_dim(cotangent, (2 * m + which) * wcols, wcols, 1)
            for m in range(pieces)
        ]
        return found[0] if pieces == 1 else jnp.concatenate(found, 1)

    kept, sent = columns_of(side), columns_of(1 - side)
    came = swap(sent, "ctx", 1)
    flip = heads // 2
    far_kept = swap(kept, "head", flip)
    far_came = swap(came, "head", flip)
    cot_pair = jnp.stack([kept, came, far_kept, far_came], 0).reshape(2, 2, tok_rows, -1)
    offsets = [0, flip]
    flip //= 2
    while flip:
        cot_pair = jnp.concatenate([cot_pair, swap(cot_pair, "head", flip)], 0)
        offsets = offsets + [o ^ flip for o in offsets]
        flip //= 2
    cot_pair = lax.optimization_barrier(cot_pair.reshape(heads, 2 * tok_rows, -1))
    slot_of = {o: i for i, o in enumerate(offsets)}

    def cot_chunk(chunk):
        relative = (chunk // pieces) ^ head_index
        slot = jnp.zeros((), jnp.int32)
        for o, i in slot_of.items():
            slot = jnp.where(relative == o, i, slot)
        part = lax.dynamic_index_in_dim(cot_pair, slot, 0, keepdims=False)
        return lax.dynamic_slice_in_dim(part, (chunk % pieces) * wcols, wcols, 1)

    def clip(index):
        return jnp.clip(index, 0, groups - 1)

    arrivals = [(out_weight, group, True)]
    rising = falling = both = out_weight
    for s in range(1, groups):
        if s > half:
            both = shift(both, groups, (s - 1, groups), (0, groups - s))
        else:
            rising = shift(rising, groups, up=(s - 1, groups))
            falling = shift(falling, groups, down=(0, groups - s))
            both = rising + falling
        below, above = group >= s, group + s < groups
        if s < half:
            arrivals += [(rising, group - s, below), (falling, group + s, above)]
        else:
            arrivals.append((both, jnp.where(below, group - s, group + s), below | above))
    all_weight = blank((groups + 1,) + out_weight.shape)
    for chunk, index, valid in arrivals:
        place = jnp.where(valid, index, groups)
        all_weight = lax.dynamic_update_index_in_dim(all_weight, chunk, place, 0)

    grad_both = 0.0
    for chunk, index, _ in arrivals[:-1]:
        grad_both += dot_nt(cot_chunk(clip(index)), chunk)
    grad_both = lax.optimization_barrier(grad_both)
    chunk, index, _ = arrivals[-1]
    part = cot_chunk(clip(index))[tok_rows:]
    grad_theirs = (grad_both[tok_rows:] + dot_nt(part, chunk)).astype(BF16)
    theirs = swap(grad_theirs, "ctx", 1)
    part = cot_chunk(clip(index))[:tok_rows]
    grad_mine = grad_both[:tok_rows] + dot_nt(part, chunk)

    column, row = picked_rows(table_index, level_table.shape[0])
    table = level_tables(level_table, level_column, levels, tok_bits + 1, ctx_bits, ctx_index)
    flipped = table.transpose(0, 2, 1)
    clear = (1 - (ctx_index >> jnp.arange(ctx_bits) & 1)).astype(F32)
    flags = jnp.ones((2, HD), F32)

    away = [o for o in range(heads) if o & 1]
    home = [o ^ 1 for o in away]
    column, row, table, flipped, flags = lax.optimization_barrier(
        (column, row, table, flipped, flags)
    )
    near = near_of(queries, keys, values, column, table)
    attn_parts = 2
    attn_heads = head_count // attn_parts
    pairs = []
    for p in range(attn_parts):
        attn = far_of(near, queries, column, table, seg_list, levels, attn_heads, p * attn_heads)
        attn_came = swap(attn, "ctx", 1)
        pairs.append(jnp.concatenate([attn, attn_came], 0))
    attn_pair = lax.optimization_barrier(jnp.concatenate(pairs, 1))

    def weight_part(index, attn):
        return lax.dot_general(
            attn, cot_chunk(clip(index)), (((0,), (0,)), ((), ())), preferred_element_type=F32
        )

    products = []
    for s in range(1, groups + 1):
        going_up, going_down = group + groups - s, group - groups + s
        if s == groups:
            wanted = [group]
        elif s <= half:
            wanted = [jnp.where(group < half, going_up, going_down)]
        else:
            wanted = [going_up, going_down]
        found = []
        if s == 1:
            for pair in pairs:
                found.append(weight_part(wanted[0], pair))
        else:
            for index in wanted:
                product = weight_part(index, attn_pair).astype(BF16)
                found.append(lax.optimization_barrier(product).astype(F32))
        products.append(found)
    up = down = both = None
    for s in range(1, groups):
        found = products[s - 1]
        apart = 2 * s < groups - 1
        if s == 1:
            rises = [x.astype(BF16) for x in found]
            rises = rises if apart else [jnp.concatenate(rises, 0)]
        elif s <= half:
            rises = [(found[0] + both.astype(F32)).astype(BF16)]
        else:
            rises = [(x + y.astype(F32)).astype(BF16) for x, y in zip(found, (up, down))]
        if apart:
            moved = []
            for rise in rises:
                moved.append(shift(rise, groups, (0, s - 1), (groups - s, groups)))
            both = moved[0] if len(moved) == 1 else jnp.concatenate(moved, 0)
        else:
            up = shift(rises[0], groups, up=(0, s - 1))
            down = shift(rises[-1], groups, down=(groups - s, groups))
    total = products[-1][0] + up.astype(F32) + down.astype(F32)
    grad_weight = total * (tok_rows * ctx_count) ** (-0.5)

    first, *pending, grad = adjoints_of(
        queries, grad_mine, theirs, row, flipped, tok_bits + 1, ctx_bits, head_count, 0
    )
    adjoint = 0.0
    for bit in range(1, ctx_bits - 1):
        one_way = bit == ctx_bits - 2
        partners = []
        for i, level in enumerate(pending[1:]):
            partners.append(swap(level, "ctx", 1 << bit, downward=one_way, within=1 << bit + 1 + i))
        partner = swap(pending[0], "ctx", 1 << bit, downward=True)
        adjoint += clear[bit] * partner.astype(F32)
        pending = [
            (x.astype(F32) + y.astype(F32)).astype(BF16) for x, y in zip(pending[1:], partners)
        ]
    for k in range(half):
        partner = post(pending[0], half, k)
        adjoint += partner.astype(F32)
    sent = (adjoint + side.astype(F32) * first.astype(F32)).astype(BF16)
    adjoint = adjoint.astype(BF16)
    adjoint_came = swap(sent, "ctx", 1)
    found = [adjoint, adjoint_came]
    parts = 1
    part_heads = head_count // parts
    nears = ()
    for p in range(parts):
        nears = tuple(
            backward_of(
                queries, keys, values, grad, column, row, table, flipped, seg_list, levels,
                part_heads, p * part_heads, nears,
            )
        )
    grad_queries, near_dk, near_dv = nears
    grad_keys, grad_values = finish_of(
        keys, values, near_dk, near_dv, found, flags, head_count, 0, ()
    )

    def layer_part(offset, i):
        chunk = (head_index ^ offset) * pieces + i
        weight = lax.dynamic_index_in_dim(all_weight, chunk, 0, keepdims=False)
        return dot_nn(attn_pair, weight)

    came = {}
    for o in away:
        for i in range(pieces):
            sent = layer_part(o, i).astype(BF16)
            came[o ^ 1, i] = swap(sent, "head", 1)
    kept = []
    for o in home:
        for i in range(pieces):
            kept.append((layer_part(o, i) + came[o, i].astype(F32)).astype(BF16))
    partials = {o: [[x] for x in kept[i * pieces : (i + 1) * pieces]] for i, o in enumerate(home)}
    flip = 2
    while flip < heads:
        out_going = sorted(o for o in partials if o & flip)
        summed = {}
        for o in out_going:
            found = []
            for i in range(pieces):
                came = swap(sum_of(partials[o][i]), "head", flip)
                found.append(partials[o ^ flip][i] + [came])
            summed[o ^ flip] = found
        partials = summed
        flip *= 2
    sent = jnp.concatenate([sum_of([t[tok_rows:] for t in terms]) for terms in partials[0]], 1)
    other = swap(sent, "ctx", 1)
    layer_out = blank((tok_rows, feature_width))
    for i, terms in enumerate(partials[0]):
        own = sum_of([t[:tok_rows] for t in terms])
        theirs = other[:, i * wcols : (i + 1) * wcols]
        for part, which in ((own, side), (theirs, 1 - side)):
            layer_out = lax.dynamic_update_slice(layer_out, part, (0, (2 * i + which) * wcols))
    return (layer_out, grad_queries, grad_keys, grad_values, grad_weight)


def solution(mesh):
    placed = (
        P("ctx", "head"),
        P("ctx", "head"),
        P("ctx", "head"),
        P("ctx", "head"),
        P("head", "ctx"),
        P(None, "head", None),
        P("ctx"),
        P(),
    )
    return jax.shard_map(
        step,
        mesh=mesh,
        in_specs=placed,
        out_specs=(
            P("ctx", "head"),
            P("ctx", "head"),
            P("ctx", "head"),
            P("ctx", "head"),
            P("head", "ctx"),
        ),
        check_vma=False,
    )
```

```python
import jax
import jax.numpy as jnp
from jax import lax
from jax.experimental import pallas as pl
from jax.experimental.pallas import tpu as pltpu
from jax.sharding import PartitionSpec as P


HD = 128
F32 = jnp.float32
BF16 = jnp.bfloat16

GRANTS = {"near": 12 << 20, "far": 12 << 20, "adjoints": 12 << 20}


def route(block, axis, pairs):
    return lax.ppermute(block, axis, pairs)


def swap(block, axis, flip, upward=False, downward=False, within=0):
    pairs = [(i, i ^ flip) for i in range(lax.axis_size(axis)) if i & within == within]
    if upward:
        pairs = [(i, j) for i, j in pairs if i < j]
    if downward:
        pairs = [(i, j) for i, j in pairs if i > j]
    return route(block, axis, pairs)


def shift(block, groups, up=None, down=None):
    pairs = []
    for step, reach in ((1, up), (-1, down)):
        if reach is None:
            continue
        for group in range(max(reach[0], 0), min(reach[1], groups - 1) + 1):
            if 0 <= group + step < groups:
                pairs += [(2 * group + side, 2 * (group + step) + side) for side in (0, 1)]
    return route(block, "ctx", pairs)


def dot_nn(a, b):
    return lax.dot_general(a, b, (((1,), (0,)), ((), ())), preferred_element_type=F32)


def dot_nt(a, b):
    return lax.dot_general(a, b, (((1,), (1,)), ((), ())), preferred_element_type=F32)


def dot_tn(a, b):
    return lax.dot_general(a, b, (((0,), (0,)), ((), ())), preferred_element_type=F32)


def post(block, source, target):
    return route(block, "ctx", [(2 * source + side, 2 * target + side) for side in (0, 1)])


def sum_of(terms):
    total = terms[0].astype(F32)
    for term in terms[1:]:
        total = total + term.astype(F32)
    return total.astype(BF16)


def halves(x):
    high = lax.reduce_precision(x, 8, 7)
    return high.astype(BF16), (x - high).astype(BF16)


def near_blocks(tok_rows):
    base = min(2 * HD, tok_rows)
    blocks = [(at, at, base, None) for at in range(0, tok_rows, base)]
    size = base
    while size < tok_rows:
        level = size.bit_length()
        blocks += [(at + size, at, size, level) for at in range(0, tok_rows, 2 * size)]
        size *= 2
    return blocks


def masks():
    row = lax.broadcasted_iota(jnp.int32, (HD, HD), 0)
    col = lax.broadcasted_iota(jnp.int32, (HD, HD), 1)
    level = jnp.zeros((HD, HD), jnp.int32)
    for bit in range(HD.bit_length() - 1):
        level = level + ((row ^ col) >= 1 << bit).astype(jnp.int32)
    return jnp.where(col <= row, level, HD - 1), level, row <= col


def tiled(tiles, flip):
    first, cross, second = tiles
    blank = jnp.zeros((HD, HD), F32)
    if flip:
        upper, lower = (first, cross), (blank, second)
    else:
        upper, lower = (first, blank), (cross, second)
    return jnp.concatenate([jnp.concatenate(upper, 1), jnp.concatenate(lower, 1)], 0)


def weight_rows(lam, row, size, level, where):
    if level is not None:
        return lam[row : row + size, level : level + 1]

    def tile(at):
        return jnp.take_along_axis(lam[at : at + HD], where[0], axis=1, mode="promise_in_bounds")

    if size == HD:
        return tile(row)
    level = HD.bit_length()
    cross = jnp.broadcast_to(lam[row + HD : row + size, level : level + 1], (HD, HD))
    return tiled((tile(row), cross, tile(row + HD)), False)


def weight_cols(lam_t, row, size, level, where):
    if level is not None:
        return lam_t[level : level + 1, row : row + size]

    def tile(at):
        found = [
            jnp.take_along_axis(
                lam_t[:8, at : at + HD], where[1][i : i + 8], axis=0, mode="promise_in_bounds"
            )
            for i in range(0, HD, 8)
        ]
        return jnp.where(where[2], jnp.concatenate(found, 0), 0.0)

    if size == HD:
        return tile(row)
    level = HD.bit_length()
    cross = jnp.broadcast_to(lam_t[level : level + 1, row + HD : row + size], (HD, HD))
    return tiled((tile(row), cross, tile(row + HD)), True)


def add_rows(total, at, part):
    for i in range(0, part.shape[0], HD):
        slot = (at + i) // HD
        piece = part[i : i + HD]
        total[slot] = piece if total[slot] is None else total[slot] + piece


def state_kernel(pack, k_ref, v_ref, o_ref):
    for n in range(pack):
        at = pl.ds(n * HD, HD)
        o_ref[n] = dot_tn(k_ref[:, at], v_ref[:, at]).astype(BF16)


def near_kernel(pack, q_ref, k_ref, v_ref, picked_ref, table_ref, o_ref):
    tok_rows = q_ref.shape[0]
    where = masks()
    for n in range(pack):
        q, k, v = (ref[:, pl.ds(n * HD, HD)] for ref in (q_ref, k_ref, v_ref))
        lam = dot_nn(picked_ref[...], table_ref[n])
        total = [None] * (tok_rows // HD)
        for row, col, size, level in near_blocks(tok_rows):
            weight = weight_rows(lam, row, size, level, where)
            score = dot_nt(q[row : row + size], k[col : col + size])
            add_rows(total, row, dot_nn((weight * score).astype(BF16), v[col : col + size]))
        for i in range(tok_rows // HD):
            o_ref[i * HD : (i + 1) * HD, pl.ds(n * HD, HD)] = total[i]


def far_kernel(pack, far, levels, near_ref, q_ref, picked_ref, table_ref, *refs):
    segs, o_ref = refs[:far], refs[far]
    for n in range(pack):
        lanes = pl.ds(n * HD, HD)
        lam = dot_nn(picked_ref[...], table_ref[n])
        through = dot_nn(q_ref[:, lanes], jnp.concatenate([seg[n] for seg in segs], 1))
        out = near_ref[:, lanes]
        for j in range(far):
            out = out + lam[:, levels + j : levels + j + 1] * through[:, j * HD : (j + 1) * HD]
        o_ref[:, lanes] = out.astype(BF16)


def adjoint_kernel(
    pack, far, near, picked_ref, q_ref, mine_ref, theirs_ref, table_ref, *refs
):
    level_refs, g_ref = refs[:far], refs[far]
    for n in range(pack):
        lanes = pl.ds(n * HD, HD)
        g = (mine_ref[:, lanes] + theirs_ref[:, lanes].astype(F32)).astype(BF16)
        g_ref[:, lanes] = g
        lam = dot_nn(table_ref[n], picked_ref[...])
        q_t = q_ref[:, lanes].T.astype(F32)
        stacked = jnp.concatenate(
            [(lam[near + j : near + j + 1] * q_t).astype(BF16) for j in range(far)], 0
        )
        found = dot_nn(stacked, g)
        for j in range(far):
            level_refs[j][n] = found[j * HD : (j + 1) * HD].astype(BF16)


def backward_kernel(
    pack, far, levels, q_ref, k_ref, v_ref, g_ref, column_ref, row_ref, table_ref, flipped_ref, *refs
):
    segs, (dq_ref, dk_ref, dv_ref) = refs[:far], refs[far:]
    tok_rows = q_ref.shape[0]
    where = masks()
    for n in range(pack):
        lanes = pl.ds(n * HD, HD)
        q_all, k_all, v_all, g_all = (ref[:, lanes] for ref in (q_ref, k_ref, v_ref, g_ref))
        lam = dot_nn(column_ref[...], table_ref[n])
        lam_t = dot_nn(flipped_ref[n], row_ref[...])
        dq, dk, dv = ([None] * (tok_rows // HD) for _ in range(3))
        for row, col, size, level in near_blocks(tok_rows):
            q, g = q_all[row : row + size], g_all[row : row + size]
            k, v = k_all[col : col + size], v_all[col : col + size]
            weight = weight_rows(lam, row, size, level, where)
            flipped = weight_cols(lam_t, row, size, level, where)
            add_rows(dq, row, dot_nn((weight * dot_nt(g, v)).astype(BF16), k))
            add_rows(dk, col, dot_nn((flipped * dot_nt(v, g)).astype(BF16), q))
            add_rows(dv, col, dot_nn((flipped * dot_nt(k, q)).astype(BF16), g))
        back = dot_nt(g_all, jnp.concatenate([seg[n] for seg in segs], 0))
        for i in range(tok_rows // HD):
            out = dq[i]
            at = i * HD
            for j in range(far):
                scale = lam[at : at + HD, levels + j : levels + j + 1]
                out = out + scale * back[at : at + HD, j * HD : (j + 1) * HD]
            dq_ref[at : at + HD, lanes] = out.astype(BF16)
            dk_ref[at : at + HD, lanes] = dk[i].astype(BF16)
            dv_ref[at : at + HD, lanes] = dv[i].astype(BF16)


def finish_kernel(pack, far, k_ref, v_ref, dk_ref, dv_ref, *refs):
    found, (dk_out, dv_out) = refs[:far], refs[far:]
    for n in range(pack):
        lanes = pl.ds(n * HD, HD)
        adjoint = found[0][n].astype(F32)
        for j in range(1, far):
            adjoint = adjoint + found[j][n].astype(F32)
        adjoint = adjoint.astype(BF16)
        dk_out[:, lanes] = (dk_ref[:, lanes].astype(F32) + dot_nt(v_ref[:, lanes], adjoint)).astype(BF16)
        dv_out[:, lanes] = (dv_ref[:, lanes].astype(F32) + dot_nn(k_ref[:, lanes], adjoint)).astype(BF16)


def shape(dims, kind):
    return jax.ShapeDtypeStruct(dims, kind)


def per_head(name, kernel, most, flops, heads, first, ins, outs, consts=(), into=()):
    pack = min(most, heads)

    def spec(x):
        if len(x.shape) == 2:
            at = first // pack if x.shape[1] > heads * HD else 0
            return pl.BlockSpec((ins[0].shape[0], pack * HD), lambda h: (0, h + at))
        at = first // pack if x.shape[-3] > heads else 0
        lead = (0,) * (len(x.shape) - 3)
        return pl.BlockSpec(x.shape[:-3] + (pack,) + x.shape[-2:], lambda h: lead + (h + at, 0, 0))

    def run(*refs):
        kernel(pack, *refs[len(into) :])

    size = flops // HD + sum(x.size * x.dtype.itemsize for x in outs)
    whole = [pl.BlockSpec(x.shape, lambda h: (0, 0)) for x in consts]
    kept = [pl.BlockSpec(memory_space=pl.ANY)] * len(into)
    single = len(outs) == 1
    return pl.pallas_call(
        run,
        grid=(heads // pack,),
        in_specs=kept + whole + [spec(x) for x in ins],
        out_specs=spec(outs[0]) if single else [spec(x) for x in outs],
        out_shape=outs[0] if single else list(outs),
        input_output_aliases={i: i for i in range(len(into))},
        compiler_params=pltpu.CompilerParams(vmem_limit_bytes=GRANTS.get(name)),
        cost_estimate=pl.CostEstimate(flops=flops, bytes_accessed=size, transcendentals=0),
    )(*into, *consts, *ins)


def states_of(keys, values):
    rows, width = keys.shape
    heads = width // HD
    return per_head(
        "states", state_kernel, 4, 2 * rows * width * HD, heads, 0,
        (keys, values), (shape((heads, HD, HD), BF16),),
    )


def near_of(queries, keys, values, column, table):
    rows, width = queries.shape

    def kernel(pack, picked, q, k, v, table, out):
        near_kernel(pack, q, k, v, picked, table, out)

    return per_head(
        "near", kernel, 2, 6 * rows * rows * width, width // HD, 0,
        (queries, keys, values, table), (shape((rows, width), F32),), (column,),
    )


def far_of(near, queries, column, table, segs, levels, heads, first):
    rows = queries.shape[0]

    def kernel(pack, picked, *refs):
        far_kernel(pack, len(segs), levels, *refs[:2], picked, *refs[2:])

    return per_head(
        "far", kernel, 2, 2 * len(segs) * rows * heads * HD * HD, heads, first,
        (near, queries, table, *segs), (shape((rows, heads * HD), BF16),), (column,),
    )


def adjoints_of(queries, mine, theirs, row, flipped, near, far, heads, first):
    rows = queries.shape[0]

    def kernel(pack, *refs):
        adjoint_kernel(pack, far, near, *refs)

    return per_head(
        "adjoints", kernel, 4, 2 * far * rows * heads * HD * HD, heads, first,
        (queries, mine, theirs, flipped),
        (shape((heads, HD, HD), BF16),) * far + (shape((rows, heads * HD), BF16),),
        (row,),
    )


def backward_of(queries, keys, values, grad, column, row, table, flipped, segs, levels, heads, first, into):
    rows, width = queries.shape

    def kernel(pack, column, row, *refs):
        backward_kernel(pack, len(segs), levels, *refs[:4], column, row, *refs[4:])

    part = shape((rows, width), BF16)
    return per_head(
        "retreat", kernel, 2, 12 * rows * rows * heads * HD, heads, first,
        (queries, keys, values, grad, table, flipped, *segs),
        (shape((rows, width), BF16), part, part), (column, row), into,
    )


def finish_of(keys, values, dk, dv, found, heads, first, into):
    rows, width = keys.shape

    def kernel(pack, *refs):
        finish_kernel(pack, len(found), *refs)

    return per_head(
        "finish", kernel, 4, 4 * rows * heads * HD * HD, heads, first,
        (keys, values, dk, dv, *found), (shape((rows, width), BF16),) * 2, (), into,
    )


def blank(dims):
    return pl.pallas_call(
        lambda o_ref: None,
        out_specs=pl.BlockSpec(memory_space=pl.ANY),
        out_shape=shape(dims, BF16),
        name="blank",
    )()


def level_scales(levels):
    level_ids = jnp.arange(levels, dtype=jnp.float32)
    return jnp.where(level_ids < 0.5, 1.0, jnp.exp2(-(level_ids - 1.0) * 0.5))


def level_tables(level_table, level_column, levels, near, ctx_bits, ctx_index):
    columns = (
        level_column[:levels, None] == jnp.arange(level_table.shape[2], dtype=jnp.int32)[None, :]
    ).astype(F32)
    scaled = columns * (level_scales(levels) * HD ** (-0.5))[:, None]
    bits = (ctx_index >> jnp.arange(ctx_bits, dtype=jnp.int32) & 1).astype(F32)
    scaled = jnp.concatenate([scaled, scaled[near:] * bits[:, None]], 0)
    table = jnp.sum(level_table.transpose(1, 0, 2)[:, :, None, :] * scaled[None, None], -1)
    table = jnp.pad(table, ((0, 0), (0, 0), (0, HD - table.shape[2])))
    high, low = halves(table)
    return jnp.concatenate([high, low], 1)


def picked_rows(table_index, table_count):
    ids = jnp.arange(2 * table_count, dtype=jnp.int32) % table_count
    column = (table_index[:, None] == ids[None, :]).astype(BF16)
    row = (table_index[None, :] == ids[:, None]).astype(BF16)
    return column, row


def step(queries, keys, values, cotangent, out_weight, level_table, table_index, level_column):
    tok_rows, feature_width = queries.shape
    head_count = feature_width // HD
    ctx_count = lax.axis_size("ctx")
    ctx_bits = ctx_count.bit_length() - 1
    tok_bits = tok_rows.bit_length() - 1
    levels = tok_bits + ctx_bits + 1
    ctx_index = lax.axis_index("ctx")
    head_index = lax.axis_index("head")
    heads = lax.axis_size("head")
    groups = ctx_count // 2
    half = groups // 2
    side = ctx_index & 1
    group = ctx_index >> 1
    wcols = out_weight.shape[1]
    pieces = feature_width // wcols // 2

    running = states_of(keys, values)
    seg_list = []
    for bit in range(ctx_bits - 1):
        seg = swap(running, "ctx", 1 << bit, upward=0 < bit == ctx_bits - 2)
        seg_list.append(seg)
        running = (running.astype(F32) + seg.astype(F32)).astype(BF16)
    seg = None
    for k in range(half):
        sent = post(running, half - 1, groups - 1 - k)
        seg = sent if seg is None else seg + sent
    seg_list.append(seg)

    def columns_of(which):
        found = [
            lax.dynamic_slice_in_dim(cotangent, (2 * m + which) * wcols, wcols, 1)
            for m in range(pieces)
        ]
        return found[0] if pieces == 1 else jnp.concatenate(found, 1)

    kept, sent = columns_of(side), columns_of(1 - side)
    came = swap(sent, "ctx", 1)
    flip = heads // 2
    far_kept = swap(kept, "head", flip)
    far_came = swap(came, "head", flip)
    cot_pair = jnp.stack([kept, came, far_kept, far_came], 0).reshape(2, 2, tok_rows, -1)
    offsets = [0, flip]
    flip //= 2
    while flip:
        cot_pair = jnp.concatenate([cot_pair, swap(cot_pair, "head", flip)], 0)
        offsets = offsets + [o ^ flip for o in offsets]
        flip //= 2
    cot_pair = lax.optimization_barrier(cot_pair.reshape(heads, 2 * tok_rows, -1))
    slot_of = {o: i for i, o in enumerate(offsets)}

    def cot_chunk(chunk):
        relative = (chunk // pieces) ^ head_index
        slot = jnp.zeros((), jnp.int32)
        for o, i in slot_of.items():
            slot = jnp.where(relative == o, i, slot)
        part = lax.dynamic_index_in_dim(cot_pair, slot, 0, keepdims=False)
        return lax.dynamic_slice_in_dim(part, (chunk % pieces) * wcols, wcols, 1)

    def clip(index):
        return jnp.clip(index, 0, groups - 1)

    arrivals = [(out_weight, group, True)]
    rising = falling = both = out_weight
    for s in range(1, groups):
        if s > half:
            both = shift(both, groups, (s - 1, groups), (0, groups - s))
        else:
            rising = shift(rising, groups, up=(s - 1, groups))
            falling = shift(falling, groups, down=(0, groups - s))
            both = rising + falling
        below, above = group >= s, group + s < groups
        if s < half:
            arrivals += [(rising, group - s, below), (falling, group + s, above)]
        else:
            arrivals.append((both, jnp.where(below, group - s, group + s), below | above))
    all_weight = blank((groups + 1,) + out_weight.shape)
    for chunk, index, valid in arrivals:
        place = jnp.where(valid, index, groups)
        all_weight = lax.dynamic_update_index_in_dim(all_weight, chunk, place, 0)

    grad_both = 0.0
    for chunk, index, _ in arrivals[:-1]:
        grad_both += dot_nt(cot_chunk(clip(index)), chunk)
    grad_both = lax.optimization_barrier(grad_both)
    chunk, index, _ = arrivals[-1]
    part = cot_chunk(clip(index))[tok_rows:]
    grad_theirs = (grad_both[tok_rows:] + dot_nt(part, chunk)).astype(BF16)
    theirs = swap(grad_theirs, "ctx", 1)
    part = cot_chunk(clip(index))[:tok_rows]
    grad_mine = grad_both[:tok_rows] + dot_nt(part, chunk)

    column, row = picked_rows(table_index, level_table.shape[0])
    table = level_tables(level_table, level_column, levels, tok_bits + 1, ctx_bits, ctx_index)
    flipped = table.transpose(0, 2, 1)
    clear = (1 - (ctx_index >> jnp.arange(ctx_bits) & 1)).astype(F32)

    away = [o for o in range(heads) if o & 1]
    home = [o ^ 1 for o in away]
    column, row, table, flipped = lax.optimization_barrier((column, row, table, flipped))
    near = near_of(queries, keys, values, column, table)
    attn_parts = 2
    attn_heads = head_count // attn_parts
    pairs = []
    for p in range(attn_parts):
        attn = far_of(near, queries, column, table, seg_list, levels, attn_heads, p * attn_heads)
        attn_came = swap(attn, "ctx", 1)
        pairs.append(jnp.concatenate([attn, attn_came], 0))
    attn_pair = lax.optimization_barrier(jnp.concatenate(pairs, 1))

    def weight_part(index, attn):
        return lax.dot_general(
            attn, cot_chunk(clip(index)), (((0,), (0,)), ((), ())), preferred_element_type=F32
        )

    products = []
    for s in range(1, groups + 1):
        going_up, going_down = group + groups - s, group - groups + s
        if s == groups:
            wanted = [group]
        elif s <= half:
            wanted = [jnp.where(group < half, going_up, going_down)]
        else:
            wanted = [going_up, going_down]
        found = []
        if s == 1:
            for pair in pairs:
                found.append(weight_part(wanted[0], pair))
        else:
            for index in wanted:
                product = weight_part(index, attn_pair).astype(BF16)
                found.append(lax.optimization_barrier(product).astype(F32))
        products.append(found)
    up = down = both = None
    for s in range(1, groups):
        found = products[s - 1]
        apart = 2 * s < groups - 1
        if s == 1:
            rises = [x.astype(BF16) for x in found]
            rises = rises if apart else [jnp.concatenate(rises, 0)]
        elif s <= half:
            rises = [(found[0] + both.astype(F32)).astype(BF16)]
        else:
            rises = [(x + y.astype(F32)).astype(BF16) for x, y in zip(found, (up, down))]
        if apart:
            moved = []
            for rise in rises:
                moved.append(shift(rise, groups, (0, s - 1), (groups - s, groups)))
            both = moved[0] if len(moved) == 1 else jnp.concatenate(moved, 0)
        else:
            up = shift(rises[0], groups, up=(0, s - 1))
            down = shift(rises[-1], groups, down=(groups - s, groups))
    total = products[-1][0] + up.astype(F32) + down.astype(F32)
    grad_weight = total * (tok_rows * ctx_count) ** (-0.5)

    first, *pending, grad = adjoints_of(
        queries, grad_mine, theirs, row, flipped, tok_bits + 1, ctx_bits, head_count, 0
    )
    adjoint = 0.0
    for bit in range(1, ctx_bits - 1):
        one_way = bit == ctx_bits - 2
        partners = []
        for i, level in enumerate(pending[1:]):
            partners.append(swap(level, "ctx", 1 << bit, downward=one_way, within=1 << bit + 1 + i))
        partner = swap(pending[0], "ctx", 1 << bit, downward=True)
        adjoint += clear[bit] * partner.astype(F32)
        pending = [
            (x.astype(F32) + y.astype(F32)).astype(BF16) for x, y in zip(pending[1:], partners)
        ]
    for k in range(half):
        partner = post(pending[0], half, k)
        adjoint += partner.astype(F32)
    sent = (adjoint + side.astype(F32) * first.astype(F32)).astype(BF16)
    adjoint = adjoint.astype(BF16)
    adjoint_came = swap(sent, "ctx", 1)
    found = [adjoint, adjoint_came]
    parts = 1
    part_heads = head_count // parts
    nears = ()
    for p in range(parts):
        nears = tuple(
            backward_of(
                queries, keys, values, grad, column, row, table, flipped, seg_list, levels,
                part_heads, p * part_heads, nears,
            )
        )
    grad_queries, near_dk, near_dv = nears
    grad_keys, grad_values = finish_of(
        keys, values, near_dk, near_dv, found, head_count, 0, ()
    )

    def layer_part(offset, i):
        chunk = (head_index ^ offset) * pieces + i
        weight = lax.dynamic_index_in_dim(all_weight, chunk, 0, keepdims=False)
        return dot_nn(attn_pair, weight)

    came = {}
    for o in away:
        for i in range(pieces):
            sent = layer_part(o, i).astype(BF16)
            came[o ^ 1, i] = swap(sent, "head", 1)
    kept = []
    for o in home:
        for i in range(pieces):
            kept.append((layer_part(o, i) + came[o, i].astype(F32)).astype(BF16))
    partials = {o: [[x] for x in kept[i * pieces : (i + 1) * pieces]] for i, o in enumerate(home)}
    flip = 2
    while flip < heads:
        out_going = sorted(o for o in partials if o & flip)
        summed = {}
        for o in out_going:
            found = []
            for i in range(pieces):
                came = swap(sum_of(partials[o][i]), "head", flip)
                found.append(partials[o ^ flip][i] + [came])
            summed[o ^ flip] = found
        partials = summed
        flip *= 2
    sent = jnp.concatenate([sum_of([t[tok_rows:] for t in terms]) for terms in partials[0]], 1)
    other = swap(sent, "ctx", 1)
    layer_out = blank((tok_rows, feature_width))
    for i, terms in enumerate(partials[0]):
        own = sum_of([t[:tok_rows] for t in terms])
        theirs = other[:, i * wcols : (i + 1) * wcols]
        for part, which in ((own, side), (theirs, 1 - side)):
            layer_out = lax.dynamic_update_slice(layer_out, part, (0, (2 * i + which) * wcols))
    return (layer_out, grad_queries, grad_keys, grad_values, grad_weight)


def solution(mesh):
    placed = (
        P("ctx", "head"),
        P("ctx", "head"),
        P("ctx", "head"),
        P("ctx", "head"),
        P("head", "ctx"),
        P(None, "head", None),
        P("ctx"),
        P(),
    )
    return jax.shard_map(
        step,
        mesh=mesh,
        in_specs=placed,
        out_specs=(
            P("ctx", "head"),
            P("ctx", "head"),
            P("ctx", "head"),
            P("ctx", "head"),
            P("head", "ctx"),
        ),
        check_vma=False,
    )
```
